128 devices in a mesh: cams: 128 (over x, y, z, core).
Axes of the slice: x: 4, y: 4, z: 4, core: 2. Of those that a mesh axis runs over, the one named last changes fastest.
Arguments:
- right_side: float32 [512, 288], P('cams')
- schur_tiles: float32 [512, 4, 288, 288], P('cams'), as said below
- block_cols: int32 [512, 4], P('cams'), may hold values from 0 to 511, as said below
- tile_counts: int32 [512], P('cams'), may hold values from 1 to 4, as said below
- jacobi_inverse: float32 [512, 288, 288], P('cams'), as said below
Outputs:
- camera_update: float32 [512, 288], P('cams')
- final_residual: float32 [512, 288], P('cams')
The draws below stay inside these ranges and needn't reach their ends.
Inputs may be any that keep to these rules, and one draw needn't show every extreme that they name: block_cols[g, 0] = g; the other slots of row g hold distinct blocks (g + o) mod 512 with 1 <= o <= 8. `tile_counts`: slot 0 is always live; some block row has all 4 slots live. `schur_tiles`: S, built from the tiles as in the reference program, is symmetric positive definite. `jacobi_inverse`: every tile is symmetric positive definite.
All inputs are finite; a program needn't handle non-finite values.
Results may differ from the reference program's by a relative error of at most 0.00025.
Values sent between devices are 32-bit elements; how exact they have to be, the bound alone decides.
A program may use at most 64 MiB of HBM per device.

```python
import jax
import jax.numpy as jnp
from jax import lax

BW = 288
NB_DEV = 4
SLOTS = 4
BAND = 2
ITERS = 2
NB = 512


def draw_right_side(key, part):
    rows = jnp.arange(NB, dtype=jnp.float32)
    ramp = 1.0 + 2.0 * rows / max(NB - 1, 1)
    first = jax.random.fold_in(jax.random.fold_in(key, 5), 0)
    base = jnp.clip(jax.random.normal(first, (NB, BW), jnp.float32), -6.0, 6.0)
    return base * ramp[:, None]


def draw_schur_tiles(key, part):
    first, second = jax.random.split(jax.random.fold_in(key, 7))
    scale = (BW * 2.0 * SLOTS) ** (-0.5)
    noise = jnp.clip(jax.random.normal(first, (NB, SLOTS, BW, BW), jnp.float32), -4.0, 4.0) * scale
    diag_vals = jax.random.uniform(second, (NB, BW), jnp.float32, 3.0, 6.0)
    eye = (lax.broadcasted_iota(jnp.int32, (BW, BW), 0) == lax.broadcasted_iota(jnp.int32, (BW, BW), 1)).astype(jnp.float32)
    centre = 0.5 * (noise[:, 0] + jnp.swapaxes(noise[:, 0], -1, -2)) + eye[None] * diag_vals[:, :, None]
    return noise.at[:, 0].set(centre)


def draw_block_cols(key, part):
    keys = jax.random.split(jax.random.fold_in(key, 3), NB)

    def one_row(row_key):
        return jnp.sort(jax.random.permutation(row_key, BAND * NB_DEV)[:SLOTS - 1]).astype(jnp.int32) + 1
    offsets = jax.vmap(one_row)(keys)
    rows = jnp.arange(NB, dtype=jnp.int32)
    ahead = (rows[:, None] + offsets) % NB
    return jnp.concatenate([rows[:, None], ahead], axis=1).astype(jnp.int32)


def draw_tile_counts(key, part):
    first, second = jax.random.split(jax.random.fold_in(key, 9))
    counts = jax.random.randint(first, (NB,), 1, SLOTS + 1)
    where_full = jax.random.randint(second, (), 0, NB)
    return counts.at[where_full].set(SLOTS).astype(jnp.int32)


def draw_jacobi_inverse(key, part):
    first, second = jax.random.split(jax.random.fold_in(key, 13))
    scale = 0.04 * BW ** (-0.5)
    noise = jnp.clip(jax.random.normal(first, (NB, BW, BW), jnp.float32), -4.0, 4.0) * scale
    diag_vals = jax.random.uniform(second, (NB, BW), jnp.float32, 0.15, 0.3)
    eye = (lax.broadcasted_iota(jnp.int32, (BW, BW), 0) == lax.broadcasted_iota(jnp.int32, (BW, BW), 1)).astype(jnp.float32)
    return 0.5 * (noise + jnp.swapaxes(noise, -1, -2)) + eye[None] * diag_vals[:, :, None]


def setup_inputs(seed: int = 0) -> dict:
    arg_keys = jax.random.split(jax.random.key(seed), 6)
    right_side = draw_right_side(jax.random.fold_in(arg_keys[5], 71), 0)
    schur_tiles = draw_schur_tiles(jax.random.fold_in(arg_keys[5], 71), 0)
    block_cols = draw_block_cols(jax.random.fold_in(arg_keys[5], 71), 0)
    tile_counts = draw_tile_counts(jax.random.fold_in(arg_keys[5], 71), 0)
    jacobi_inverse = draw_jacobi_inverse(jax.random.fold_in(arg_keys[5], 71), 0)
    return {"right_side": right_side, "schur_tiles": schur_tiles, "block_cols": block_cols, "tile_counts": tile_counts, "jacobi_inverse": jacobi_inverse}


HIGH = lax.Precision.HIGHEST


def apply_system(schur_tiles, block_cols, tile_counts, vector):
    blocks, slots = block_cols.shape
    slot_ids = lax.broadcasted_iota(jnp.int32, (blocks, slots), 1)
    live = slot_ids < tile_counts[:, None]
    picked = vector[block_cols]
    upper = jnp.einsum("bsij,bsj->bsi", schur_tiles, picked, precision=HIGH)
    result = jnp.sum(jnp.where(live[:, :, None], upper, jnp.float32(0.0)), axis=1)
    lower = jnp.einsum("bsij,bi->bsj", schur_tiles, vector, precision=HIGH)
    lower = jnp.where((live & (slot_ids > 0))[:, :, None], lower, jnp.float32(0.0))
    spread = jnp.zeros_like(vector).at[block_cols.reshape(-1)].add(lower.reshape(blocks * slots, -1))
    return result + spread


def apply_precond(jacobi_inverse, vector):
    return jnp.einsum("bij,bj->bi", jacobi_inverse, vector, precision=HIGH)


def reference(right_side, schur_tiles, block_cols, tile_counts, jacobi_inverse):
    camera_update = jnp.zeros_like(right_side)
    final_residual = right_side
    precond = apply_precond(jacobi_inverse, final_residual)
    norm_now = jnp.sum(final_residual * precond)
    direction = precond
    for iteration in range(ITERS):
        image = apply_system(schur_tiles, block_cols, tile_counts, direction)
        alpha = norm_now / jnp.sum(direction * image)
        camera_update = camera_update + alpha * direction
        final_residual = final_residual - alpha * image
        if iteration + 1 < ITERS:
            precond = apply_precond(jacobi_inverse, final_residual)
            fresh = jnp.sum(final_residual * precond)
            direction = precond + (fresh / norm_now) * direction
            norm_now = fresh
    return camera_update, final_residual
```

```python
import functools

import jax
import jax.numpy as jnp
from jax import lax
from jax.experimental import pallas as pl
from jax.experimental.pallas import tpu as pltpu
from jax.sharding import PartitionSpec as P

MESH = pl.DeviceIdType.MESH
LANES = 128
ROWS = 32
NEAR = 8
BAND = 2
AXIS = "cams"


def lane_groups(width):
    return [(start, min(start + LANES, width)) for start in range(0, width, LANES)]


def fold_rows(value):
    rows, width = value.shape
    return jnp.sum(value.reshape(rows // 8, 8, width), axis=0)


def kernel(
    n,
    rhs_hbm,
    tiles_hbm,
    cols_hbm,
    counts_hbm,
    minv_hbm,
    x_out,
    r_out,
    tiles,
    minv,
    rhs,
    cols,
    counts,
    p_col,
    q_col,
    p_ext,
    q_ext,
    s_row,
    w_row,
    prods,
    p_low,
    q_low,
    p_got,
    q_got,
    near_buf,
    far_buf,
    tile_sem,
    minv_sem,
    small_sem,
    halo_send,
    halo_recv,
    near_send,
    near_recv,
    far_send,
    far_recv,
):
    blocks, slots, width, _ = tiles.shape
    far = n // NEAR
    me = lax.axis_index(AXIS)
    mine = lax.rem(me, NEAR)
    plane = lax.div(me, NEAR)
    groups = lane_groups(width)
    chunks = width // ROWS

    small = [
        pltpu.make_async_copy(rhs_hbm, rhs, small_sem.at[0]),
        pltpu.make_async_copy(cols_hbm, cols, small_sem.at[1]),
        pltpu.make_async_copy(counts_hbm, counts, small_sem.at[2]),
    ]
    minv_copy = [
        pltpu.make_async_copy(minv_hbm.at[g], minv.at[g], minv_sem.at[g]) for g in range(blocks)
    ]
    tile_copy = {
        (g, k): pltpu.make_async_copy(
            tiles_hbm.at[g, k], tiles.at[g, k], tile_sem.at[g * slots + k]
        )
        for g in range(blocks)
        for k in range(slots)
    }
    small[0].start()
    for copy in minv_copy:
        copy.start()
    small[1].start()
    small[2].start()
    for k in list(range(1, slots)) + [0]:
        for g in range(blocks):
            tile_copy[g, k].start()

    def ahead(steps):
        return (lax.rem(me + n + steps, n),)

    def near_peer(steps):
        return (plane * NEAR + lax.rem(mine + NEAR + steps, NEAR),)

    def far_peer(steps):
        return (lax.rem(plane + far + steps, far) * NEAR + mine,)

    barrier = pltpu.get_barrier_semaphore()
    peers = [ahead(s) for s in (1, -1, 2, -2)]
    peers += [near_peer(s) for s in range(1, NEAR)]
    peers += [far_peer(s) for s in range(1, far)]
    for peer in peers:
        pl.semaphore_signal(barrier, inc=1, device_id=peer, device_id_type=MESH)

    def send(index, source, target, steps):
        return pltpu.make_async_remote_copy(
            src_ref=source,
            dst_ref=target,
            send_sem=halo_send.at[index],
            recv_sem=halo_recv.at[index],
            device_id=ahead(steps),
            device_id_type=MESH,
        )

    def eye(chunk):
        offset = (chunk * ROWS) % LANES
        lane = lax.broadcasted_iota(jnp.int32, (ROWS, LANES), 1)
        row = lax.broadcasted_iota(jnp.int32, (ROWS, LANES), 0)
        return lane == row + offset

    eyes = [eye(c) for c in range(LANES // ROWS)]

    def times_rows(terms, column, row_out):
        sums = [jnp.zeros((8, LANES), jnp.float32) for _ in groups]
        for c in range(chunks):
            rows = slice(c * ROWS, (c + 1) * ROWS)
            total = None
            for matrix, vector in terms:
                part = matrix[rows, :] * vector
                total = part if total is None else total + part
            value = jnp.sum(total, axis=1, keepdims=True)
            wide = jnp.broadcast_to(value, (ROWS, LANES))
            if column is not None:
                column[rows, :] = wide
            at = c * ROWS // LANES
            sums[at] = sums[at] + fold_rows(jnp.where(eyes[c % len(eyes)], wide, 0.0))
        for (low, high), value in zip(groups, sums):
            row_out[:, low:high] = jnp.sum(value, axis=0, keepdims=True)[:, : high - low]

    def times_columns(matrices, column, row_outs):
        sums = [[None for _ in groups] for _ in matrices]
        for c in range(chunks):
            rows = slice(c * ROWS, (c + 1) * ROWS)
            wide = column[rows, :]
            for index, matrix in enumerate(matrices):
                for at, (low, high) in enumerate(groups):
                    part = fold_rows(matrix[rows, low:high] * wide[:, : high - low])
                    before = sums[index][at]
                    sums[index][at] = part if before is None else before + part
        for index, row_out in enumerate(row_outs):
            for (low, high), value in zip(groups, sums[index]):
                row_out[:, low:high] = jnp.sum(value, axis=0, keepdims=True)

    small[0].wait()
    for g in range(blocks):
        minv_copy[g].wait()
        times_rows(
            [(minv.at[g], rhs[g : g + 1, :])], p_col.at[g], p_ext.at[0, g : g + 1, :]
        )

    pl.semaphore_wait(barrier, len(peers))
    p_sends = [send(d - 1, p_ext.at[0], p_ext.at[d], -d) for d in range(1, BAND + 1)]
    for copy in p_sends:
        copy.start()

    small[1].wait()
    small[2].wait()
    total_blocks = n * blocks
    places = {}
    lives = {}
    for g in range(blocks):
        for k in range(1, slots):
            local = lax.rem(cols[g, k] - me * blocks + total_blocks, total_blocks)
            live = k < counts[g]
            places[g, k] = jnp.where(live, local, 0)
            lives[g, k] = live

    row_ids = lax.broadcasted_iota(jnp.int32, (blocks, width), 0)

    def spread(distance):
        total = jnp.zeros((blocks, width), jnp.float32)
        for (g, k), place in places.items():
            slot = g * slots + k
            hit = row_ids == jnp.where(lives[g, k], place - distance * blocks, -1)
            total = total + jnp.where(hit, prods[slot : slot + 1, :], 0.0)
        return total

    def picked(ext, g, k):
        place = places[g, k]
        row = ext[lax.div(place, blocks), pl.ds(lax.rem(place, blocks), 1), :]
        return jnp.where(lives[g, k], row, 0.0)

    def slot_row(g, k):
        slot = g * slots + k
        return prods.at[slot : slot + 1, :]

    for g in range(blocks):
        for k in range(1, slots):
            tile_copy[g, k].wait()
        times_columns(
            [tiles.at[g, k] for k in range(1, slots)],
            p_col.at[g],
            [slot_row(g, k) for k in range(1, slots)],
        )
    for d in range(1, BAND + 1):
        p_low[d] = spread(d)
    low_sends = [send(BAND + d - 1, p_low.at[d], p_got.at[d], d) for d in range(1, BAND + 1)]
    for copy in low_sends:
        copy.start()
    p_low[0] = spread(0)

    for g in range(blocks):
        tile_copy[g, 0].wait()
    for copy in p_sends:
        copy.wait_recv()
    for g in range(blocks):
        terms = [(tiles.at[g, 0], p_ext[0, g : g + 1, :])]
        terms += [(tiles.at[g, k], picked(p_ext, g, k)) for k in range(1, slots)]
        times_rows(terms, None, s_row.at[g : g + 1, :])
    s_near = s_row[...] + p_low[0]
    for copy in low_sends:
        copy.wait_recv()
    s_row[...] = s_near + p_got[1] + p_got[2]

    for g in range(blocks):
        times_rows(
            [(minv.at[g], s_row[g : g + 1, :])], q_col.at[g], q_ext.at[0, g : g + 1, :]
        )
    q_sends = [send(2 * BAND + d - 1, q_ext.at[0], q_ext.at[d], -d) for d in range(1, BAND + 1)]
    for copy in q_sends:
        copy.start()

    near_mine = near_buf.at[mine]

    def put_dot(index, value):
        whole = jnp.sum(value, axis=0, keepdims=True)
        total = whole[:, 0:LANES]
        for low, high in groups[1:]:
            if high - low == LANES:
                total = total + whole[:, low:high]
        near_mine[index : index + 1, :] = total
        low, high = groups[-1]
        if high - low < LANES:
            near_mine[index : index + 1, 0 : high - low] = (
                total[:, 0 : high - low] + whole[:, low:high]
            )

    put_dot(0, rhs[...] * p_ext[0])
    put_dot(1, p_ext[0] * s_row[...])
    put_dot(2, s_row[...] * q_ext[0])

    for g in range(blocks):
        times_columns(
            [tiles.at[g, k] for k in range(slots)],
            q_col.at[g],
            [slot_row(g, k) for k in range(slots)],
        )
    for d in range(1, BAND + 1):
        q_low[d] = spread(d)
    q_low_sends = [
        send(3 * BAND + d - 1, q_low.at[d], q_got.at[d], d) for d in range(1, BAND + 1)
    ]
    for copy in q_low_sends:
        copy.start()
    q_low[0] = spread(0)
    for g in range(blocks):
        w_row[g : g + 1, :] = slot_row(g, 0)[...]
    w_row[...] = w_row[...] + q_low[0]
    own = q_ext[0] * w_row[...]

    for copy in q_sends:
        copy.wait_recv()
    cross = jnp.zeros((1, width), jnp.float32)
    for d in range(1, BAND + 1):
        cross = cross + jnp.sum(q_ext[d] * q_low[d], axis=0, keepdims=True)
    diag = jnp.zeros((1, width), jnp.float32)
    for g in range(blocks):
        diag = diag + slot_row(g, 0)[...] * q_ext[0, g : g + 1, :]
    inner = jnp.sum(own, axis=0, keepdims=True)
    put_dot(3, 2.0 * (cross + inner) - diag)

    near_sends = []
    for d in range(1, NEAR):
        near_sends.append(
            pltpu.make_async_remote_copy(
                src_ref=near_mine,
                dst_ref=near_mine,
                send_sem=near_send.at[d],
                recv_sem=near_recv.at[d],
                device_id=near_peer(d),
                device_id_type=MESH,
            )
        )
    for copy in near_sends:
        copy.start()
    for copy in near_sends:
        copy.wait_recv()
    far_mine = far_buf.at[plane]
    far_mine[...] = jnp.sum(near_buf[...], axis=0)
    far_sends = []
    for d in range(1, far):
        far_sends.append(
            pltpu.make_async_remote_copy(
                src_ref=far_mine,
                dst_ref=far_mine,
                send_sem=far_send.at[d],
                recv_sem=far_recv.at[d],
                device_id=far_peer(d),
                device_id_type=MESH,
            )
        )
    for copy in far_sends:
        copy.start()

    for g in range(blocks):
        terms = [(tiles.at[g, k], picked(q_ext, g, k)) for k in range(1, slots)]
        times_rows(terms, None, s_row_up(prods, g))
    up = prods[0:blocks, :]
    for copy in q_low_sends:
        copy.wait_recv()
    w_row[...] = w_row[...] + up + q_got[1] + q_got[2]

    for copy in far_sends:
        copy.wait_recv()
    sums = jnp.sum(jnp.sum(far_buf[...], axis=0), axis=1, keepdims=True)
    sums = jnp.broadcast_to(sums, (sums.shape[0], width))
    rz, ps, sq, qw = [sums[i : i + 1, :] for i in range(4)]
    alpha = rz / ps
    fresh = rz - 2.0 * alpha * ps + alpha * alpha * sq
    grow = 1.0 + fresh / rz
    energy = grow * grow * ps - 2.0 * grow * alpha * sq + alpha * alpha * qw
    second = fresh / energy
    x_out[...] = (alpha + second * grow) * p_ext[0] - second * alpha * q_ext[0]
    r_out[...] = rhs[...] - (alpha + second * grow) * s_row[...] + second * alpha * w_row[...]

    for copy in p_sends + low_sends + q_sends + q_low_sends + near_sends + far_sends:
        copy.wait_send()


def s_row_up(ref, g):
    return ref.at[g : g + 1, :]


def solution(mesh):
    n = mesh.shape[AXIS]

    def on_device(right_side, schur_tiles, block_cols, tile_counts, jacobi_inverse):
        blocks, slots, width, _ = schur_tiles.shape
        dma = pltpu.SemaphoreType.DMA
        row = jax.ShapeDtypeStruct((blocks, width), jnp.float32)

        def vmem(*shape):
            return pltpu.VMEM(shape, jnp.float32)

        any_spec = pl.BlockSpec(memory_space=pl.ANY)
        vmem_spec = pl.BlockSpec(memory_space=pltpu.VMEM)
        return pl.pallas_call(
            functools.partial(kernel, n),
            out_shape=(row, row),
            in_specs=[any_spec] * 5,
            out_specs=(vmem_spec, vmem_spec),
            scratch_shapes=[
                vmem(blocks, slots, width, width),
                vmem(blocks, width, width),
                vmem(blocks, width),
                pltpu.SMEM((blocks, slots), jnp.int32),
                pltpu.SMEM((blocks,), jnp.int32),
                vmem(blocks, width, LANES),
                vmem(blocks, width, LANES),
                vmem(BAND + 1, blocks, width),
                vmem(BAND + 1, blocks, width),
                vmem(blocks, width),
                vmem(blocks, width),
                vmem(blocks * slots, width),
                vmem(BAND + 1, blocks, width),
                vmem(BAND + 1, blocks, width),
                vmem(BAND + 1, blocks, width),
                vmem(BAND + 1, blocks, width),
                vmem(NEAR, 4, LANES),
                vmem(n // NEAR, 4, LANES),
                dma((blocks * slots,)),
                dma((blocks,)),
                dma((3,)),
                dma((4 * BAND,)),
                dma((4 * BAND,)),
                dma((NEAR,)),
                dma((NEAR,)),
                dma((n // NEAR,)),
                dma((n // NEAR,)),
            ],
            compiler_params=pltpu.CompilerParams(
                collective_id=0, has_side_effects=True, vmem_limit_bytes=60 << 20
            ),
        )(right_side, schur_tiles, block_cols, tile_counts, jacobi_inverse)

    return jax.shard_map(
        on_device,
        mesh=mesh,
        in_specs=(
            P(AXIS, None),
            P(AXIS, None, None, None),
            P(AXIS, None),
            P(AXIS),
            P(AXIS, None, None),
        ),
        out_specs=(P(AXIS, None), P(AXIS, None)),
        check_vma=False,
    )
```

```python
import functools
import itertools

import jax
import jax.numpy as jnp
from jax import lax
from jax.experimental import pallas as pl
from jax.experimental.pallas import tpu as pltpu
from jax.sharding import PartitionSpec as P

MESH = pl.DeviceIdType.MESH
LANES = 128
ROWS = 32
NEAR = 8
BAND = 2
DOTS = 4
SIZES = {128: (4, 4, 4, 2), 16: (1, 2, 4, 2)}
AXIS = "cams"


def lane_groups(width):
    return [(start, min(start + LANES, width)) for start in range(0, width, LANES)]


def fold_rows(value):
    rows, width = value.shape
    return jnp.sum(value.reshape(rows // 8, 8, width), axis=0)


def all_peers(n, me):
    sizes = SIZES[n]
    moved, stride = [], n
    for size in sizes:
        stride //= size
        place = lax.rem(lax.div(me, stride), size)
        moved.append([lax.rem(place + step, size) * stride for step in range(size)])
    offsets = list(itertools.product(*[range(size) for size in sizes]))[1:]

    def hops(offset):
        return sum(min(o, s - o) for o, s in zip(offset[:-1], sizes[:-1])) + 0.1 * offset[-1]

    for offset in sorted(offsets, key=hops, reverse=True):
        yield sum(axis[step] for axis, step in zip(moved[1:], offset[1:])) + moved[0][offset[0]]


def kernel(
    n,
    rhs_hbm,
    tiles_hbm,
    cols_hbm,
    counts_hbm,
    minv_hbm,
    p_out,
    q_out,
    s_out,
    w_out,
    rhs_out,
    one_out,
    two_out,
    tiles,
    minv,
    rhs,
    cols,
    counts,
    p_col,
    q_col,
    p_ext,
    q_ext,
    s_row,
    w_row,
    prods,
    p_low,
    q_low,
    p_got,
    q_got,
    dots,
    everyone,
    tile_sem,
    minv_sem,
    small_sem,
    halo_send,
    halo_recv,
    all_send,
    all_recv,
    ready,
):
    blocks, slots, width, _ = tiles.shape
    far = n // NEAR
    me = lax.axis_index(AXIS)
    mine = lax.rem(me, NEAR)
    plane = lax.div(me, NEAR)
    groups = lane_groups(width)
    chunks = width // ROWS

    small = [
        pltpu.make_async_copy(rhs_hbm, rhs, small_sem.at[0]),
        pltpu.make_async_copy(cols_hbm, cols, small_sem.at[1]),
        pltpu.make_async_copy(counts_hbm, counts, small_sem.at[2]),
    ]
    minv_copy = [
        pltpu.make_async_copy(minv_hbm.at[g], minv.at[g], minv_sem.at[g]) for g in range(blocks)
    ]
    tile_copy = {
        (g, k): pltpu.make_async_copy(
            tiles_hbm.at[g, k], tiles.at[g, k], tile_sem.at[g * slots + k]
        )
        for g in range(blocks)
        for k in range(slots)
    }
    small[0].start()
    for copy in minv_copy:
        copy.start()
    small[1].start()
    small[2].start()

    def ahead(steps):
        return (lax.rem(me + n + steps, n),)

    def near_peer(steps):
        return (plane * NEAR + lax.rem(mine + NEAR + steps, NEAR),)

    def far_peer(steps):
        return (lax.rem(plane + far + steps, far) * NEAR + mine,)

    barrier = pltpu.get_barrier_semaphore()
    peers = [ahead(s) for s in (1, -1, 2, -2)]
    peers += [near_peer(s) for s in range(1, NEAR)]
    peers += [far_peer(s) for s in range(1, far)]
    for peer in peers:
        pl.semaphore_signal(barrier, inc=1, device_id=peer, device_id_type=MESH)

    def send(index, source, target, steps):
        return pltpu.make_async_remote_copy(
            src_ref=source,
            dst_ref=target,
            send_sem=halo_send.at[index],
            recv_sem=halo_recv.at[index],
            device_id=ahead(steps),
            device_id_type=MESH,
        )

    def eye(chunk):
        offset = (chunk * ROWS) % LANES
        lane = lax.broadcasted_iota(jnp.int32, (ROWS, LANES), 1)
        row = lax.broadcasted_iota(jnp.int32, (ROWS, LANES), 0)
        return lane == row + offset

    eyes = [eye(c) for c in range(LANES // ROWS)]

    def times_rows(terms, column, row_out):
        sums = [jnp.zeros((8, LANES), jnp.float32) for _ in groups]
        for c in range(chunks):
            rows = slice(c * ROWS, (c + 1) * ROWS)
            total = None
            for matrix, vector in terms:
                part = matrix[rows, :] * vector
                total = part if total is None else total + part
            value = jnp.sum(total, axis=1, keepdims=True)
            wide = jnp.broadcast_to(value, (ROWS, LANES))
            if column is not None:
                column[rows, :] = wide
            at = c * ROWS // LANES
            sums[at] = sums[at] + fold_rows(jnp.where(eyes[c % len(eyes)], wide, 0.0))
        for (low, high), value in zip(groups, sums):
            row_out[:, low:high] = jnp.sum(value, axis=0, keepdims=True)[:, : high - low]

    def times_columns(matrices, column, row_outs):
        sums = [[None for _ in groups] for _ in matrices]
        for c in range(chunks):
            rows = slice(c * ROWS, (c + 1) * ROWS)
            wide = column[rows, :]
            for index, matrix in enumerate(matrices):
                for at, (low, high) in enumerate(groups):
                    part = fold_rows(matrix[rows, low:high] * wide[:, : high - low])
                    before = sums[index][at]
                    sums[index][at] = part if before is None else before + part
        for index, row_out in enumerate(row_outs):
            for (low, high), value in zip(groups, sums[index]):
                row_out[:, low:high] = jnp.sum(value, axis=0, keepdims=True)

    small[0].wait()
    minv_copy[0].wait()
    for g in range(blocks):
        for k in range(1, slots):
            tile_copy[g, k].start()
    for g in range(blocks):
        tile_copy[g, 0].start()
    for g in range(blocks):
        if g > 0:
            minv_copy[g].wait()
        times_rows(
            [(minv.at[g], rhs[g : g + 1, :])], p_col.at[g], p_ext.at[0, g : g + 1, :]
        )

    pl.semaphore_wait(barrier, len(peers))
    for d in range(1, NEAR):
        pl.semaphore_signal(ready, inc=1, device_id=near_peer(d), device_id_type=MESH)
    p_sends = [send(d - 1, p_ext.at[0], p_ext.at[d], -d) for d in range(1, BAND + 1)]
    for copy in p_sends:
        copy.start()

    small[1].wait()
    small[2].wait()
    total_blocks = n * blocks
    places = {}
    lives = {}
    for g in range(blocks):
        for k in range(1, slots):
            local = lax.rem(cols[g, k] - me * blocks + total_blocks, total_blocks)
            live = k < counts[g]
            places[g, k] = jnp.where(live, local, 0)
            lives[g, k] = live

    row_ids = lax.broadcasted_iota(jnp.int32, (blocks, width), 0)

    def spread(distance):
        total = jnp.zeros((blocks, width), jnp.float32)
        for (g, k), place in places.items():
            slot = g * slots + k
            hit = row_ids == jnp.where(lives[g, k], place - distance * blocks, -1)
            total = total + jnp.where(hit, prods[slot : slot + 1, :], 0.0)
        return total

    def picked(ext, g, k):
        place = places[g, k]
        row = ext[lax.div(place, blocks), pl.ds(lax.rem(place, blocks), 1), :]
        return jnp.where(lives[g, k], row, 0.0)

    def slot_row(g, k):
        slot = g * slots + k
        return prods.at[slot : slot + 1, :]

    for g in range(blocks):
        for k in range(1, slots):
            tile_copy[g, k].wait()
        times_columns(
            [tiles.at[g, k] for k in range(1, slots)],
            p_col.at[g],
            [slot_row(g, k) for k in range(1, slots)],
        )
    for d in range(1, BAND + 1):
        p_low[d] = spread(d)
    low_sends = [send(BAND + d - 1, p_low.at[d], p_got.at[d], d) for d in range(1, BAND + 1)]
    for copy in low_sends:
        copy.start()
    p_low[0] = spread(0)

    for g in range(blocks):
        tile_copy[g, 0].wait()
    for copy in p_sends:
        copy.wait_recv()
    for g in range(blocks):
        terms = [(tiles.at[g, 0], p_ext[0, g : g + 1, :])]
        terms += [(tiles.at[g, k], picked(p_ext, g, k)) for k in range(1, slots)]
        times_rows(terms, None, s_row.at[g : g + 1, :])
    s_near = s_row[...] + p_low[0]
    for copy in low_sends:
        copy.wait_recv()
    s_row[...] = s_near + p_got[1] + p_got[2]

    for g in range(blocks):
        times_rows(
            [(minv.at[g], s_row[g : g + 1, :])], q_col.at[g], q_ext.at[0, g : g + 1, :]
        )
    q_sends = [send(2 * BAND + d - 1, q_ext.at[0], q_ext.at[d], -d) for d in range(1, BAND + 1)]
    for copy in q_sends:
        copy.start()

    def put_dot(index, value):
        whole = jnp.sum(jnp.sum(value, axis=0, keepdims=True), axis=1, keepdims=True)
        dots[index : index + 1, :] = jnp.broadcast_to(whole, (1, LANES))

    put_dot(0, rhs[...] * p_ext[0])
    put_dot(1, p_ext[0] * s_row[...])
    put_dot(2, s_row[...] * q_ext[0])

    for g in range(blocks):
        times_columns(
            [tiles.at[g, k] for k in range(slots)],
            q_col.at[g],
            [slot_row(g, k) for k in range(slots)],
        )
    for d in range(1, BAND + 1):
        q_low[d] = spread(d)
    q_low_sends = [
        send(3 * BAND + d - 1, q_low.at[d], q_got.at[d], d) for d in range(1, BAND + 1)
    ]
    for copy in q_low_sends:
        copy.start()
    q_low[0] = spread(0)
    for g in range(blocks):
        w_row[g : g + 1, :] = slot_row(g, 0)[...]
    w_row[...] = w_row[...] + q_low[0]
    own = q_ext[0] * w_row[...]

    for copy in q_sends:
        copy.wait_recv()
    cross = jnp.zeros((1, width), jnp.float32)
    for d in range(1, BAND + 1):
        cross = cross + jnp.sum(q_ext[d] * q_low[d], axis=0, keepdims=True)
    diag = jnp.zeros((1, width), jnp.float32)
    for g in range(blocks):
        diag = diag + slot_row(g, 0)[...] * q_ext[0, g : g + 1, :]
    inner = jnp.sum(own, axis=0, keepdims=True)
    put_dot(3, 2.0 * (cross + inner) - diag)

    lane = lax.broadcasted_iota(jnp.int32, (1, LANES), 1)
    mixed = dots[0:1, :]
    for index in range(1, DOTS):
        mixed = jnp.where(lane < index * (LANES // DOTS), mixed, dots[index : index + 1, :])
    everyone[me] = mixed
    pl.semaphore_wait(ready, NEAR - 1)
    for peer in all_peers(n, me):
        pltpu.make_async_remote_copy(
            src_ref=everyone.at[me],
            dst_ref=everyone.at[me],
            send_sem=all_send,
            recv_sem=all_recv,
            device_id=(peer,),
            device_id_type=MESH,
        ).start()
    others = everyone.at[pl.ds(0, n - 1)]

    p_out[...] = p_ext[0]
    q_out[...] = q_ext[0]
    s_out[...] = s_row[...]
    rhs_out[...] = rhs[...]
    for g in range(blocks):
        terms = [(tiles.at[g, k], picked(q_ext, g, k)) for k in range(1, slots)]
        times_rows(terms, None, s_row_up(prods, g))
    up = prods[0:blocks, :]
    for copy in q_low_sends:
        copy.wait_recv()
    w_row[...] = w_row[...] + up + q_got[1] + q_got[2]

    pltpu.make_async_copy(others, others, all_recv).wait()
    sums = jnp.sum(everyone[...], axis=0)

    def dot(index):
        first = lane == index * (LANES // DOTS)
        total = jnp.sum(jnp.where(first, sums, 0.0), axis=1, keepdims=True)
        return jnp.broadcast_to(total, (blocks, width))

    rz, ps, sq, qw = [dot(index) for index in range(DOTS)]
    alpha = rz / ps
    fresh = rz - 2.0 * alpha * ps + alpha * alpha * sq
    grow = 1.0 + fresh / rz
    energy = grow * grow * ps - 2.0 * grow * alpha * sq + alpha * alpha * qw
    second = fresh / energy
    one_out[...] = alpha + second * grow
    two_out[...] = second * alpha
    w_out[...] = w_row[...]

    for copy in p_sends + low_sends + q_sends + q_low_sends:
        copy.wait_send()
    pltpu.make_async_copy(others, others, all_send).wait()


def s_row_up(ref, g):
    return ref.at[g : g + 1, :]


def solution(mesh):
    n = mesh.shape[AXIS]

    def on_device(right_side, schur_tiles, block_cols, tile_counts, jacobi_inverse):
        blocks, slots, width, _ = schur_tiles.shape
        dma = pltpu.SemaphoreType.DMA

        def vmem(*shape):
            return pltpu.VMEM(shape, jnp.float32)

        any_spec = pl.BlockSpec(memory_space=pl.ANY)
        vmem_spec = pl.BlockSpec(memory_space=pltpu.VMEM)
        p, q, s, w, rhs, one, two = pl.pallas_call(
            functools.partial(kernel, n),
            out_shape=[vmem(blocks, width)] * 7,
            in_specs=[any_spec] * 5,
            out_specs=[vmem_spec] * 7,
            scratch_shapes=[
                vmem(blocks, slots, width, width),
                vmem(blocks, width, width),
                vmem(blocks, width),
                pltpu.SMEM((blocks, slots), jnp.int32),
                pltpu.SMEM((blocks,), jnp.int32),
                vmem(blocks, width, LANES),
                vmem(blocks, width, LANES),
                vmem(BAND + 1, blocks, width),
                vmem(BAND + 1, blocks, width),
                vmem(blocks, width),
                vmem(blocks, width),
                vmem(blocks * slots, width),
                vmem(BAND + 1, blocks, width),
                vmem(BAND + 1, blocks, width),
                vmem(BAND + 1, blocks, width),
                vmem(BAND + 1, blocks, width),
                vmem(DOTS, LANES),
                vmem(n, 1, LANES),
                dma((blocks * slots,)),
                dma((blocks,)),
                dma((3,)),
                dma((4 * BAND,)),
                dma((4 * BAND,)),
                dma(()),
                dma(()),
                pltpu.SemaphoreType.REGULAR,
            ],
            compiler_params=pltpu.CompilerParams(
                collective_id=0, has_side_effects=True, vmem_limit_bytes=60 << 20
            ),
        )(right_side, schur_tiles, block_cols, tile_counts, jacobi_inverse)
        return one * p - two * q, rhs - one * s + two * w

    return jax.shard_map(
        on_device,
        mesh=mesh,
        in_specs=(
            P(AXIS, None),
            P(AXIS, None, None, None),
            P(AXIS, None),
            P(AXIS),
            P(AXIS, None, None),
        ),
        out_specs=(P(AXIS, None), P(AXIS, None)),
        check_vma=False,
    )
```

```python
import functools
import itertools

import jax
import jax.numpy as jnp
from jax import lax
from jax.experimental import pallas as pl
from jax.experimental.pallas import tpu as pltpu
from jax.sharding import PartitionSpec as P

MESH = pl.DeviceIdType.MESH
LANES = 128
ROWS = 32
NEAR = 8
BAND = 2
DOTS = 4
SIZES = {128: (4, 4, 4, 2), 16: (1, 2, 4, 2)}
AXIS = "cams"


def lane_groups(width):
    return [(start, min(start + LANES, width)) for start in range(0, width, LANES)]


def fold_rows(value):
    rows, width = value.shape
    return jnp.sum(value.reshape(rows // 8, 8, width), axis=0)


def two_sum(a, b):
    total = a + b
    part = total - a
    return total, (a - (total - part)) + (b - part)


def split(a):
    wide = 4097.0 * a
    high = wide - (wide - a)
    return high, a - high


def two_product(a, b):
    product = a * b
    a_high, a_low = split(a)
    b_high, b_low = split(b)
    error = ((a_high * b_high - product) + a_high * b_low + a_low * b_high) + a_low * b_low
    return product, error


def sum_pairs(ref):
    parts = [(ref[at : at + 8, :], None) for at in range(0, ref.shape[0], 8)]

    def add(first, second):
        total, error = two_sum(first[0], second[0])
        for extra in (first[1], second[1]):
            error = error if extra is None else error + extra
        return total, error

    while len(parts) > 1:
        parts = [add(parts[i], parts[i + 1]) for i in range(0, len(parts), 2)]
    part = parts[0]
    for shift in (4, 2, 1):
        part = add(part, tuple(pltpu.roll(half, shift, 0) for half in part))
    return part[0][0:1, :], part[1][0:1, :]


def all_peers(n, me):
    sizes = SIZES[n]
    moved, stride = [], n
    for size in sizes:
        stride //= size
        place = lax.rem(lax.div(me, stride), size)
        moved.append([lax.rem(place + step, size) * stride for step in range(size)])
    offsets = list(itertools.product(*[range(size) for size in sizes]))[1:]

    def hops(offset):
        return sum(min(o, s - o) for o, s in zip(offset[:-1], sizes[:-1])) + 0.1 * offset[-1]

    for offset in sorted(offsets, key=hops, reverse=True):
        yield sum(axis[step] for axis, step in zip(moved[1:], offset[1:])) + moved[0][offset[0]]


def kernel(
    n,
    rhs_hbm,
    tiles_hbm,
    cols_hbm,
    counts_hbm,
    minv_hbm,
    p_out,
    q_out,
    s_out,
    w_out,
    rhs_out,
    one_out,
    two_out,
    tiles,
    minv,
    rhs,
    cols,
    counts,
    p_col,
    q_col,
    p_ext,
    q_ext,
    s_row,
    w_row,
    prods,
    p_low,
    q_low,
    p_got,
    q_got,
    dots,
    cross,
    mid_q,
    mid_low,
    everyone,
    tile_sem,
    minv_sem,
    small_sem,
    halo_send,
    halo_recv,
    mid_send,
    mid_recv,
    all_send,
    all_recv,
    ready,
):
    blocks, slots, width, _ = tiles.shape
    far = n // NEAR
    me = lax.axis_index(AXIS)
    mine = lax.rem(me, NEAR)
    plane = lax.div(me, NEAR)
    groups = lane_groups(width)
    chunks = width // ROWS

    small = [
        pltpu.make_async_copy(rhs_hbm, rhs, small_sem.at[0]),
        pltpu.make_async_copy(cols_hbm, cols, small_sem.at[1]),
        pltpu.make_async_copy(counts_hbm, counts, small_sem.at[2]),
    ]
    minv_copy = [
        pltpu.make_async_copy(minv_hbm.at[g], minv.at[g], minv_sem.at[g]) for g in range(blocks)
    ]
    tile_copy = {
        (g, k): pltpu.make_async_copy(
            tiles_hbm.at[g, k], tiles.at[g, k], tile_sem.at[g * slots + k]
        )
        for g in range(blocks)
        for k in range(slots)
    }
    small[0].start()
    for copy in minv_copy:
        copy.start()
    small[1].start()
    small[2].start()

    def ahead(steps):
        return (lax.rem(me + n + steps, n),)

    def near_peer(steps):
        return (plane * NEAR + lax.rem(mine + NEAR + steps, NEAR),)

    def far_peer(steps):
        return (lax.rem(plane + far + steps, far) * NEAR + mine,)

    barrier = pltpu.get_barrier_semaphore()
    peers = [ahead(s) for s in (1, -1, 2, -2)]
    peers += [near_peer(s) for s in range(1, NEAR)]
    peers += [far_peer(s) for s in range(1, far)]
    for peer in peers:
        pl.semaphore_signal(barrier, inc=1, device_id=peer, device_id_type=MESH)

    def send(index, source, target, steps):
        return pltpu.make_async_remote_copy(
            src_ref=source,
            dst_ref=target,
            send_sem=halo_send.at[index],
            recv_sem=halo_recv.at[index],
            device_id=ahead(steps),
            device_id_type=MESH,
        )

    def eye(chunk):
        offset = (chunk * ROWS) % LANES
        lane = lax.broadcasted_iota(jnp.int32, (ROWS, LANES), 1)
        row = lax.broadcasted_iota(jnp.int32, (ROWS, LANES), 0)
        return lane == row + offset

    eyes = [eye(c) for c in range(LANES // ROWS)]

    def times_rows(terms, column, row_out):
        sums = [jnp.zeros((8, LANES), jnp.float32) for _ in groups]
        for c in range(chunks):
            rows = slice(c * ROWS, (c + 1) * ROWS)
            total = None
            for matrix, vector in terms:
                part = matrix[rows, :] * vector
                total = part if total is None else total + part
            value = jnp.sum(total, axis=1, keepdims=True)
            wide = jnp.broadcast_to(value, (ROWS, LANES))
            if column is not None:
                column[rows, :] = wide
            at = c * ROWS // LANES
            sums[at] = sums[at] + fold_rows(jnp.where(eyes[c % len(eyes)], wide, 0.0))
        for (low, high), value in zip(groups, sums):
            row_out[:, low:high] = jnp.sum(value, axis=0, keepdims=True)[:, : high - low]

    def times_columns(matrices, column, row_outs):
        sums = [[None for _ in groups] for _ in matrices]
        for c in range(chunks):
            rows = slice(c * ROWS, (c + 1) * ROWS)
            wide = column[rows, :]
            for index, matrix in enumerate(matrices):
                for at, (low, high) in enumerate(groups):
                    part = fold_rows(matrix[rows, low:high] * wide[:, : high - low])
                    before = sums[index][at]
                    sums[index][at] = part if before is None else before + part
        for index, row_out in enumerate(row_outs):
            for (low, high), value in zip(groups, sums[index]):
                row_out[:, low:high] = jnp.sum(value, axis=0, keepdims=True)

    small[0].wait()
    minv_copy[0].wait()
    for g in range(blocks):
        for k in range(1, slots):
            tile_copy[g, k].start()
    for g in range(blocks):
        tile_copy[g, 0].start()
    for g in range(blocks):
        if g > 0:
            minv_copy[g].wait()
        times_rows(
            [(minv.at[g], rhs[g : g + 1, :])], p_col.at[g], p_ext.at[0, g : g + 1, :]
        )

    pl.semaphore_wait(barrier, len(peers))
    for d in range(1, NEAR):
        pl.semaphore_signal(ready, inc=1, device_id=near_peer(d), device_id_type=MESH)
    p_sends = [send(d - 1, p_ext.at[0], p_ext.at[d], -d) for d in range(1, BAND + 1)]
    for copy in p_sends:
        copy.start()

    small[1].wait()
    small[2].wait()
    total_blocks = n * blocks
    places = {}
    lives = {}
    for g in range(blocks):
        for k in range(1, slots):
            local = lax.rem(cols[g, k] - me * blocks + total_blocks, total_blocks)
            live = k < counts[g]
            places[g, k] = jnp.where(live, local, 0)
            lives[g, k] = live

    row_ids = lax.broadcasted_iota(jnp.int32, (blocks, width), 0)

    def spread(distance):
        total = jnp.zeros((blocks, width), jnp.float32)
        for (g, k), place in places.items():
            slot = g * slots + k
            hit = row_ids == jnp.where(lives[g, k], place - distance * blocks, -1)
            total = total + jnp.where(hit, prods[slot : slot + 1, :], 0.0)
        return total

    def picked(ext, g, k):
        place = places[g, k]
        row = ext[lax.div(place, blocks), pl.ds(lax.rem(place, blocks), 1), :]
        return jnp.where(lives[g, k], row, 0.0)

    def slot_row(g, k):
        slot = g * slots + k
        return prods.at[slot : slot + 1, :]

    for g in range(blocks):
        for k in range(1, slots):
            tile_copy[g, k].wait()
        times_columns(
            [tiles.at[g, k] for k in range(1, slots)],
            p_col.at[g],
            [slot_row(g, k) for k in range(1, slots)],
        )
    for d in range(1, BAND + 1):
        p_low[d] = spread(d)
    low_sends = [send(BAND + d - 1, p_low.at[d], p_got.at[d], d) for d in range(1, BAND + 1)]
    for copy in low_sends:
        copy.start()
    p_low[0] = spread(0)

    for g in range(blocks):
        tile_copy[g, 0].wait()
        times_columns([tiles.at[g, 0]], p_col.at[g], [w_row.at[g : g + 1, :]])
    w_row[...] = w_row[...] + p_low[0]
    for copy in p_sends:
        copy.wait_recv()
    for g in range(blocks):
        terms = [(tiles.at[g, k], picked(p_ext, g, k)) for k in range(1, slots)]
        times_rows(terms, None, s_row.at[g : g + 1, :])
    s_near = s_row[...] + w_row[...]
    for copy in low_sends:
        copy.wait_recv()
    s_row[...] = s_near + p_got[1] + p_got[2]

    for g in range(blocks):
        times_rows(
            [(minv.at[g], s_row[g : g + 1, :])], q_col.at[g], q_ext.at[0, g : g + 1, :]
        )
    q_sends = [send(2 * BAND + d - 1, q_ext.at[0], q_ext.at[d], -d) for d in range(1, BAND + 1)]
    for copy in q_sends:
        copy.start()

    def halfway(index, source, target, peer):
        return pltpu.make_async_remote_copy(
            src_ref=source,
            dst_ref=target,
            send_sem=mid_send.at[index],
            recv_sem=mid_recv.at[index],
            device_id=peer,
            device_id_type=MESH,
        )

    def halfway_q():
        return halfway(0, q_ext.at[0], mid_q, ahead(-NEAR))

    def halfway_low(distance, place):
        return halfway(
            distance, q_low.at[distance], mid_low.at[distance], (plane * NEAR + place,)
        )

    @pl.when(mine < BAND)
    def _():
        halfway_q().start()


    def put_dot(index, value):
        whole = jnp.sum(jnp.sum(value, axis=0, keepdims=True), axis=1, keepdims=True)
        dots[index : index + 1, :] = jnp.broadcast_to(whole, (1, LANES))

    put_dot(0, rhs[...] * p_ext[0])
    put_dot(1, p_ext[0] * s_row[...])
    put_dot(2, s_row[...] * q_ext[0])

    for g in range(blocks):
        times_columns(
            [tiles.at[g, k] for k in range(1, slots)],
            q_col.at[g],
            [slot_row(g, k) for k in range(1, slots)],
        )
    for d in range(1, BAND + 1):
        q_low[d] = spread(d)

    @pl.when(mine == NEAR - 1)
    def _():
        halfway_low(1, 0).start()
        halfway_low(2, 1).start()

    @pl.when(mine == NEAR - 2)
    def _():
        halfway_low(2, 0).start()

    q_low_sends = [
        send(3 * BAND + d - 1, q_low.at[d], q_got.at[d], d) for d in range(1, BAND + 1)
    ]
    for copy in q_low_sends:
        copy.start()
    q_low[0] = spread(0)
    for g in range(blocks):
        times_columns([tiles.at[g, 0]], q_col.at[g], [w_row.at[g : g + 1, :]])
    cross[...] = jnp.sum(
        q_ext[0] * (2.0 * q_low[0] + w_row[...]), axis=0, keepdims=True
    )
    w_row[...] = w_row[...] + q_low[0]

    def add_cross(rows, low):
        cross[...] = cross[...] + 2.0 * jnp.sum(rows * low, axis=0, keepdims=True)

    @pl.when(mine < NEAR - 1)
    def _():
        q_sends[0].wait_recv()
        add_cross(q_ext[1], q_low[1])

    @pl.when(mine < NEAR - 2)
    def _():
        q_sends[1].wait_recv()
        add_cross(q_ext[2], q_low[2])

    @pl.when(mine == 0)
    def _():
        halfway_q().wait_recv()
        halfway_low(1, 0).wait_recv()
        halfway_low(2, 0).wait_recv()
        add_cross(mid_q[...], mid_low[1] + mid_low[2])

    @pl.when(mine == 1)
    def _():
        halfway_q().wait_recv()
        halfway_low(2, 0).wait_recv()
        add_cross(mid_q[...], mid_low[2])

    put_dot(3, cross[...])
    lane = lax.broadcasted_iota(jnp.int32, (1, LANES), 1)
    mixed = dots[0:1, :]
    for index in range(1, DOTS):
        mixed = jnp.where(lane < index * (LANES // DOTS), mixed, dots[index : index + 1, :])
    everyone[pl.ds(me, 1), :] = mixed
    pl.semaphore_wait(ready, NEAR - 1)
    for peer in all_peers(n, me):
        pltpu.make_async_remote_copy(
            src_ref=everyone.at[pl.ds(me, 1), :],
            dst_ref=everyone.at[pl.ds(me, 1), :],
            send_sem=all_send,
            recv_sem=all_recv,
            device_id=(peer,),
            device_id_type=MESH,
        ).start()
    others = everyone.at[pl.ds(0, n - 1), :]

    p_out[...] = p_ext[0]
    q_out[...] = q_ext[0]
    s_out[...] = s_row[...]
    rhs_out[...] = rhs[...]
    @pl.when(mine >= NEAR - 1)
    def _():
        q_sends[0].wait_recv()

    @pl.when(mine >= NEAR - 2)
    def _():
        q_sends[1].wait_recv()

    for g in range(blocks):
        terms = [(tiles.at[g, k], picked(q_ext, g, k)) for k in range(1, slots)]
        times_rows(terms, None, s_row_up(prods, g))
    up = prods[0:blocks, :]
    for copy in q_low_sends:
        copy.wait_recv()
    w_row[...] = w_row[...] + up + q_got[1] + q_got[2]

    pltpu.make_async_copy(others, others, all_recv).wait()
    high, low = sum_pairs(everyone)

    def dot(index):
        first = lane == index * (LANES // DOTS)
        return [
            jnp.sum(jnp.where(first, part, 0.0), axis=1, keepdims=True) for part in (high, low)
        ]

    (rz, rz_low), (ps, ps_low), (sq, sq_low), (qw, qw_low) = [dot(i) for i in range(DOTS)]

    def ratio(top, top_low):
        value = top / ps
        product, error = two_product(value, ps)
        return value, ((top - product) - error + (top_low - value * ps_low)) / ps

    alpha, alpha_low = ratio(rz, rz_low)
    gamma, gamma_low = ratio(sq, sq_low)
    product, error = two_product(alpha, sq)
    upper = (product - ps) + (error + (alpha * sq_low - ps_low) + alpha_low * sq)
    product, error = two_product(gamma, sq)
    lower = (qw - product) - (error - qw_low + gamma * sq_low + gamma_low * sq)
    two = upper / lower
    one = alpha + two * gamma
    one_out[...] = jnp.broadcast_to(one, (blocks, width))
    two_out[...] = jnp.broadcast_to(two, (blocks, width))
    w_out[...] = w_row[...]

    for copy in p_sends + low_sends + q_sends + q_low_sends:
        copy.wait_send()
    pltpu.make_async_copy(others, others, all_send).wait()

    @pl.when(mine < BAND)
    def _():
        halfway_q().wait_send()

    @pl.when(mine == NEAR - 1)
    def _():
        halfway_low(1, 0).wait_send()

    @pl.when(mine >= NEAR - 2)
    def _():
        halfway_low(2, 0).wait_send()


def s_row_up(ref, g):
    return ref.at[g : g + 1, :]


def solution(mesh):
    n = mesh.shape[AXIS]

    def on_device(right_side, schur_tiles, block_cols, tile_counts, jacobi_inverse):
        blocks, slots, width, _ = schur_tiles.shape
        dma = pltpu.SemaphoreType.DMA

        def vmem(*shape):
            return pltpu.VMEM(shape, jnp.float32)

        any_spec = pl.BlockSpec(memory_space=pl.ANY)
        vmem_spec = pl.BlockSpec(memory_space=pltpu.VMEM)
        p, q, s, w, rhs, one, two = pl.pallas_call(
            functools.partial(kernel, n),
            out_shape=[vmem(blocks, width)] * 7,
            in_specs=[any_spec] * 5,
            out_specs=[vmem_spec] * 7,
            scratch_shapes=[
                vmem(blocks, slots, width, width),
                vmem(blocks, width, width),
                vmem(blocks, width),
                pltpu.SMEM((blocks, slots), jnp.int32),
                pltpu.SMEM((blocks,), jnp.int32),
                vmem(blocks, width, LANES),
                vmem(blocks, width, LANES),
                vmem(BAND + 1, blocks, width),
                vmem(BAND + 1, blocks, width),
                vmem(blocks, width),
                vmem(blocks, width),
                vmem(blocks * slots, width),
                vmem(BAND + 1, blocks, width),
                vmem(BAND + 1, blocks, width),
                vmem(BAND + 1, blocks, width),
                vmem(BAND + 1, blocks, width),
                vmem(DOTS, LANES),
                vmem(1, width),
                vmem(blocks, width),
                vmem(BAND + 1, blocks, width),
                vmem(n, LANES),
                dma((blocks * slots,)),
                dma((blocks,)),
                dma((3,)),
                dma((4 * BAND,)),
                dma((4 * BAND,)),
                dma((BAND + 1,)),
                dma((BAND + 1,)),
                dma(()),
                dma(()),
                pltpu.SemaphoreType.REGULAR,
            ],
            compiler_params=pltpu.CompilerParams(
                collective_id=0, has_side_effects=True, vmem_limit_bytes=60 << 20
            ),
        )(right_side, schur_tiles, block_cols, tile_counts, jacobi_inverse)
        return one * p - two * q, rhs - one * s + two * w

    return jax.shard_map(
        on_device,
        mesh=mesh,
        in_specs=(
            P(AXIS, None),
            P(AXIS, None, None, None),
            P(AXIS, None),
            P(AXIS),
            P(AXIS, None, None),
        ),
        out_specs=(P(AXIS, None), P(AXIS, None)),
        check_vma=False,
    )
```

```python
import functools
import itertools

import jax
import jax.numpy as jnp
from jax import lax
from jax.experimental import pallas as pl
from jax.experimental.pallas import tpu as pltpu
from jax.sharding import PartitionSpec as P

MESH = pl.DeviceIdType.MESH
LANES = 128
ROWS = 32
NEAR = 8
BAND = 2
DOTS = 4
SIZES = {128: (4, 4, 4, 2), 16: (1, 2, 4, 2)}
AXIS = "cams"


def lane_groups(width):
    return [(start, min(start + LANES, width)) for start in range(0, width, LANES)]


def fold_rows(value):
    rows, width = value.shape
    return jnp.sum(value.reshape(rows // 8, 8, width), axis=0)


def two_sum(a, b):
    total = a + b
    part = total - a
    return total, (a - (total - part)) + (b - part)


def split(a):
    wide = 4097.0 * a
    high = wide - (wide - a)
    return high, a - high


def two_product(a, b):
    product = a * b
    a_high, a_low = split(a)
    b_high, b_low = split(b)
    error = ((a_high * b_high - product) + a_high * b_low + a_low * b_high) + a_low * b_low
    return product, error


def sum_pairs(ref):
    parts = [(ref[at : at + 8, :], None) for at in range(0, ref.shape[0], 8)]

    def add(first, second):
        total, error = two_sum(first[0], second[0])
        for extra in (first[1], second[1]):
            error = error if extra is None else error + extra
        return total, error

    while len(parts) > 1:
        parts = [add(parts[i], parts[i + 1]) for i in range(0, len(parts), 2)]
    part = parts[0]
    for shift in (4, 2, 1):
        part = add(part, tuple(pltpu.roll(half, shift, 0) for half in part))
    return part[0][0:1, :], part[1][0:1, :]


def all_peers(n, me):
    sizes = SIZES[n]
    moved, stride = [], n
    for size in sizes:
        stride //= size
        place = lax.rem(lax.div(me, stride), size)
        moved.append([lax.rem(place + step, size) * stride for step in range(size)])
    offsets = list(itertools.product(*[range(size) for size in sizes]))[1:]

    def hops(offset):
        return sum(min(o, s - o) for o, s in zip(offset[:-1], sizes[:-1])) + 0.1 * offset[-1]

    for offset in sorted(offsets, key=hops):
        yield sum(axis[step] for axis, step in zip(moved[1:], offset[1:])) + moved[0][offset[0]]


def kernel(
    n,
    rhs_hbm,
    tiles_hbm,
    cols_hbm,
    counts_hbm,
    minv_hbm,
    p_out,
    q_out,
    s_out,
    w_out,
    rhs_out,
    one_out,
    two_out,
    tiles,
    minv,
    rhs,
    cols,
    counts,
    p_col,
    q_col,
    p_ext,
    q_ext,
    s_row,
    w_row,
    prods,
    p_low,
    q_low,
    p_got,
    q_got,
    dots,
    cross,
    mid_p,
    everyone,
    tile_sem,
    minv_sem,
    small_sem,
    halo_send,
    halo_recv,
    mid_send,
    mid_recv,
    all_send,
    all_recv,
    ready,
):
    blocks, slots, width, _ = tiles.shape
    far = n // NEAR
    me = lax.axis_index(AXIS)
    mine = lax.rem(me, NEAR)
    plane = lax.div(me, NEAR)
    groups = lane_groups(width)
    chunks = width // ROWS

    small = [
        pltpu.make_async_copy(rhs_hbm, rhs, small_sem.at[0]),
        pltpu.make_async_copy(cols_hbm, cols, small_sem.at[1]),
        pltpu.make_async_copy(counts_hbm, counts, small_sem.at[2]),
    ]
    minv_copy = [
        pltpu.make_async_copy(minv_hbm.at[g], minv.at[g], minv_sem.at[g]) for g in range(blocks)
    ]
    tile_copy = {
        (g, k): pltpu.make_async_copy(
            tiles_hbm.at[g, k], tiles.at[g, k], tile_sem.at[g * slots + k]
        )
        for g in range(blocks)
        for k in range(slots)
    }
    def start_tiles(g):
        for k in range(1, slots):
            tile_copy[g, k].start()

    small[0].start()
    for copy in minv_copy:
        copy.start()
    start_tiles(0)

    def ahead(steps):
        return (lax.rem(me + n + steps, n),)

    def near_peer(steps):
        return (plane * NEAR + lax.rem(mine + NEAR + steps, NEAR),)

    def far_peer(steps):
        return (lax.rem(plane + far + steps, far) * NEAR + mine,)

    def ring_peers(axis):
        size = SIZES[n][axis]
        stride = 1 if axis == 1 else SIZES[n][1]
        place = lax.rem(lax.div(plane, stride), size)
        for step in range(1, size):
            moved = plane + (lax.rem(place + step, size) - place) * stride
            yield (moved * NEAR + mine,)

    line = lax.rem(plane, SIZES[n][1])
    first = line == 0
    last = line == SIZES[n][1] - 1
    relayed = first & (mine < BAND)

    barrier = pltpu.get_barrier_semaphore()

    def enter(peer):
        pl.semaphore_signal(barrier, inc=1, device_id=peer, device_id_type=MESH)

    @pl.when(mine == 0)
    def _():
        enter(ahead(-1))

    @pl.when(mine < BAND)
    def _():
        enter(ahead(-2))

    @pl.when(last & (mine < BAND))
    def _():
        enter(ahead(NEAR))

    @pl.when(jnp.logical_not(last) & (mine >= NEAR - 2))
    def _():
        enter(ahead(2))

    @pl.when(jnp.logical_not(last) & (mine == NEAR - 1))
    def _():
        enter(ahead(1))

    peers = [near_peer(s) for s in range(1, NEAR)]
    peers += [*ring_peers(0), *ring_peers(1)]
    for peer in peers:
        enter(peer)
    links = jnp.where(mine == 0, jnp.where(first, 1, 2), 0) + jnp.where(mine == 1, 1, 0)
    links = links + jnp.where(mine == NEAR - 2, 1, 0) + jnp.where(mine == NEAR - 1, 2, 0)

    def send(index, source, target, steps):
        return pltpu.make_async_remote_copy(
            src_ref=source,
            dst_ref=target,
            send_sem=halo_send.at[index],
            recv_sem=halo_recv.at[index],
            device_id=ahead(steps),
            device_id_type=MESH,
        )

    def eye(chunk):
        offset = (chunk * ROWS) % LANES
        lane = lax.broadcasted_iota(jnp.int32, (ROWS, LANES), 1)
        row = lax.broadcasted_iota(jnp.int32, (ROWS, LANES), 0)
        return lane == row + offset

    eyes = [eye(c) for c in range(LANES // ROWS)]

    def times_rows(terms, column, row_out):
        sums = [jnp.zeros((8, LANES), jnp.float32) for _ in groups]
        for c in range(chunks):
            rows = slice(c * ROWS, (c + 1) * ROWS)
            total = None
            for matrix, vector in terms:
                part = matrix[rows, :] * vector
                total = part if total is None else total + part
            value = jnp.sum(total, axis=1, keepdims=True)
            wide = jnp.broadcast_to(value, (ROWS, LANES))
            if column is not None:
                column[rows, :] = wide
            at = c * ROWS // LANES
            sums[at] = sums[at] + fold_rows(jnp.where(eyes[c % len(eyes)], wide, 0.0))
        for (low, high), value in zip(groups, sums):
            row_out[:, low:high] = jnp.sum(value, axis=0, keepdims=True)[:, : high - low]

    def times_columns(matrices, column, row_outs):
        sums = [[None for _ in groups] for _ in matrices]
        for c in range(chunks):
            rows = slice(c * ROWS, (c + 1) * ROWS)
            wide = column[rows, :]
            for index, matrix in enumerate(matrices):
                for at, (low, high) in enumerate(groups):
                    part = fold_rows(matrix[rows, low:high] * wide[:, : high - low])
                    before = sums[index][at]
                    sums[index][at] = part if before is None else before + part
        for index, row_out in enumerate(row_outs):
            for (low, high), value in zip(groups, sums[index]):
                row_out[:, low:high] = jnp.sum(value, axis=0, keepdims=True)

    start_tiles(1)
    small[1].start()
    small[2].start()
    small[0].wait()
    for g in range(blocks):
        minv_copy[g].wait()
        if g + 2 < blocks:
            start_tiles(g + 2)
        times_rows(
            [(minv.at[g], rhs[g : g + 1, :])], p_col.at[g], p_ext.at[0, g : g + 1, :]
        )

    pl.semaphore_wait(barrier, len(peers) + links)
    p_sends = [send(d - 1, p_ext.at[0], p_ext.at[d], -d) for d in range(1, BAND + 1)]

    def relay(index, source, target, recv, peer):
        return pltpu.make_async_remote_copy(
            src_ref=source,
            dst_ref=target,
            send_sem=mid_send.at[index],
            recv_sem=recv,
            device_id=peer,
            device_id_type=MESH,
        )

    def relay_in():
        return relay(0, p_ext.at[0], mid_p, mid_recv, ahead(-NEAR))

    def relay_out(distance, place):
        return relay(
            distance,
            mid_p,
            p_ext.at[distance],
            halo_recv.at[distance - 1],
            (plane * NEAR + place,),
        )

    @pl.when(relayed)
    def _():
        relay_in().start()

    direct = [jnp.logical_not(first & (mine < d)) for d in range(1, BAND + 1)]
    for copy, sent in zip(p_sends, direct):

        @pl.when(sent)
        def _(copy=copy):
            copy.start()

    for peer in ring_peers(1):
        pl.semaphore_signal(ready.at[0], inc=1, device_id=peer, device_id_type=MESH)

    small[1].wait()
    small[2].wait()
    total_blocks = n * blocks
    places = {}
    lives = {}
    for g in range(blocks):
        for k in range(1, slots):
            local = lax.rem(cols[g, k] - me * blocks + total_blocks, total_blocks)
            live = k < counts[g]
            places[g, k] = jnp.where(live, local, 0)
            lives[g, k] = live

    row_ids = lax.broadcasted_iota(jnp.int32, (blocks, width), 0)

    def spread(distance):
        total = jnp.zeros((blocks, width), jnp.float32)
        for (g, k), place in places.items():
            slot = g * slots + k
            hit = row_ids == jnp.where(lives[g, k], place - distance * blocks, -1)
            total = total + jnp.where(hit, prods[slot : slot + 1, :], 0.0)
        return total

    def picked(ext, g, k):
        place = places[g, k]
        row = ext[lax.div(place, blocks), pl.ds(lax.rem(place, blocks), 1), :]
        return jnp.where(lives[g, k], row, 0.0)

    def slot_row(g, k):
        slot = g * slots + k
        return prods.at[slot : slot + 1, :]

    for g in range(blocks):
        for k in range(1, slots):
            tile_copy[g, k].wait()
        tile_copy[g, 0].start()
        times_columns(
            [tiles.at[g, k] for k in range(1, slots)],
            p_col.at[g],
            [slot_row(g, k) for k in range(1, slots)],
        )
    for d in range(1, BAND + 1):
        p_low[d] = spread(d)
    low_sends = [send(BAND + d - 1, p_low.at[d], p_got.at[d], d) for d in range(1, BAND + 1)]
    for copy in low_sends:
        copy.start()
    p_low[0] = spread(0)

    @pl.when(last & (mine == 0))
    def _():
        relay_in().wait_recv()
        relay_out(1, NEAR - 1).start()
        relay_out(2, NEAR - 2).start()

    @pl.when(last & (mine == 1))
    def _():
        relay_in().wait_recv()
        relay_out(2, NEAR - 1).start()

    for copy in p_sends:
        copy.wait_recv()
    for g in range(blocks):
        terms = [(tiles.at[g, k], picked(p_ext, g, k)) for k in range(1, slots)]
        times_rows(terms, None, s_row.at[g : g + 1, :])
    for g in range(blocks):
        tile_copy[g, 0].wait()
        times_columns([tiles.at[g, 0]], p_col.at[g], [w_row.at[g : g + 1, :]])
    w_row[...] = w_row[...] + p_low[0]
    s_near = s_row[...] + w_row[...]
    pl.semaphore_wait(ready.at[0], SIZES[n][1] - 1)
    for d in range(1, NEAR):
        pl.semaphore_signal(ready.at[1], inc=1, device_id=near_peer(d), device_id_type=MESH)
    for copy in low_sends:
        copy.wait_recv()
    s_row[...] = s_near + p_got[1] + p_got[2]

    for g in range(blocks):
        times_rows(
            [(minv.at[g], s_row[g : g + 1, :])], q_col.at[g], q_ext.at[0, g : g + 1, :]
        )
    q_sends = [send(2 * BAND + d - 1, q_ext.at[0], q_ext.at[d], -d) for d in range(1, BAND + 1)]
    for copy in q_sends:
        copy.start()

    def put_dot(index, value):
        whole = jnp.sum(jnp.sum(value, axis=0, keepdims=True), axis=1, keepdims=True)
        dots[index : index + 1, :] = jnp.broadcast_to(whole, (1, LANES))

    put_dot(0, rhs[...] * p_ext[0])
    put_dot(1, p_ext[0] * s_row[...])
    put_dot(2, s_row[...] * q_ext[0])

    for g in range(blocks):
        times_columns(
            [tiles.at[g, k] for k in range(1, slots)],
            q_col.at[g],
            [slot_row(g, k) for k in range(1, slots)],
        )
    for d in range(1, BAND + 1):
        q_low[d] = spread(d)

    q_low_sends = [
        send(3 * BAND + d - 1, q_low.at[d], q_got.at[d], d) for d in range(1, BAND + 1)
    ]
    for copy in q_low_sends:
        copy.start()
    q_low[0] = spread(0)
    for g in range(blocks):
        times_columns([tiles.at[g, 0]], q_col.at[g], [w_row.at[g : g + 1, :]])
    cross[...] = jnp.sum(
        q_ext[0] * (2.0 * q_low[0] + w_row[...]), axis=0, keepdims=True
    )
    w_row[...] = w_row[...] + q_low[0]

    def add_cross(rows, low):
        cross[...] = cross[...] + 2.0 * jnp.sum(rows * low, axis=0, keepdims=True)

    here = [(mine < NEAR - 3) | (mine == NEAR - 2), mine < NEAR - 4]
    both_there = (mine == 0) | (mine == NEAR - 2)
    one_there = (mine == 1) | (mine == NEAR - 1)
    got_there = [both_there, both_there | one_there]
    for copy, wanted, d in zip(q_sends, here, range(1, BAND + 1)):

        @pl.when(wanted)
        def _(copy=copy, d=d):
            copy.wait_recv()
            add_cross(q_ext[d], q_low[d])

    for copy, wanted, d in zip(q_low_sends, got_there, range(1, BAND + 1)):

        @pl.when(wanted)
        def _(copy=copy, d=d):
            copy.wait_recv()
            add_cross(q_ext[0], q_got[d])

    put_dot(3, cross[...])
    lane = lax.broadcasted_iota(jnp.int32, (1, LANES), 1)
    mixed = dots[0:1, :]
    for index in range(1, DOTS):
        mixed = jnp.where(lane < index * (LANES // DOTS), mixed, dots[index : index + 1, :])
    everyone[pl.ds(me, 1), :] = mixed
    pl.semaphore_wait(ready.at[1], NEAR - 1)
    for peer in all_peers(n, me):
        pltpu.make_async_remote_copy(
            src_ref=everyone.at[pl.ds(me, 1), :],
            dst_ref=everyone.at[pl.ds(me, 1), :],
            send_sem=all_send,
            recv_sem=all_recv,
            device_id=(peer,),
            device_id_type=MESH,
        ).start()
    others = everyone.at[pl.ds(0, n - 1), :]

    p_out[...] = p_ext[0]
    q_out[...] = q_ext[0]
    s_out[...] = s_row[...]
    rhs_out[...] = rhs[...]
    for copy, wanted in zip(q_sends, here):

        @pl.when(jnp.logical_not(wanted))
        def _(copy=copy):
            copy.wait_recv()

    for g in range(blocks):
        terms = [(tiles.at[g, k], picked(q_ext, g, k)) for k in range(1, slots)]
        times_rows(terms, None, s_row_up(prods, g))
    up = prods[0:blocks, :]
    for copy, wanted in zip(q_low_sends, got_there):

        @pl.when(jnp.logical_not(wanted))
        def _(copy=copy):
            copy.wait_recv()

    w_row[...] = w_row[...] + up + q_got[1] + q_got[2]

    pltpu.make_async_copy(others, others, all_recv).wait()
    high, low = sum_pairs(everyone)

    def dot(index):
        first = lane == index * (LANES // DOTS)
        return [
            jnp.sum(jnp.where(first, part, 0.0), axis=1, keepdims=True) for part in (high, low)
        ]

    (rz, rz_low), (ps, ps_low), (sq, sq_low), (qw, qw_low) = [dot(i) for i in range(DOTS)]

    def ratio(top, top_low):
        value = top / ps
        product, error = two_product(value, ps)
        return value, ((top - product) - error + (top_low - value * ps_low)) / ps

    alpha, alpha_low = ratio(rz, rz_low)
    gamma, gamma_low = ratio(sq, sq_low)
    product, error = two_product(alpha, sq)
    upper = (product - ps) + (error + (alpha * sq_low - ps_low) + alpha_low * sq)
    product, error = two_product(gamma, sq)
    lower = (qw - product) - (error - qw_low + gamma * sq_low + gamma_low * sq)
    two = upper / lower
    one = alpha + two * gamma
    one_out[...] = jnp.broadcast_to(one, (blocks, width))
    two_out[...] = jnp.broadcast_to(two, (blocks, width))
    w_out[...] = w_row[...]

    for copy in low_sends + q_sends + q_low_sends:
        copy.wait_send()
    pltpu.make_async_copy(others, others, all_send).wait()

    for copy, sent in zip(p_sends, direct):

        @pl.when(sent)
        def _(copy=copy):
            copy.wait_send()

    @pl.when(relayed)
    def _():
        relay_in().wait_send()

    @pl.when(last & (mine == 0))
    def _():
        relay_out(1, NEAR - 1).wait_send()
        relay_out(2, NEAR - 2).wait_send()

    @pl.when(last & (mine == 1))
    def _():
        relay_out(2, NEAR - 1).wait_send()


def s_row_up(ref, g):
    return ref.at[g : g + 1, :]


def solution(mesh):
    n = mesh.shape[AXIS]

    def on_device(right_side, schur_tiles, block_cols, tile_counts, jacobi_inverse):
        blocks, slots, width, _ = schur_tiles.shape
        dma = pltpu.SemaphoreType.DMA

        def vmem(*shape):
            return pltpu.VMEM(shape, jnp.float32)

        any_spec = pl.BlockSpec(memory_space=pl.ANY)
        vmem_spec = pl.BlockSpec(memory_space=pltpu.VMEM)
        p, q, s, w, rhs, one, two = pl.pallas_call(
            functools.partial(kernel, n),
            out_shape=[vmem(blocks, width)] * 7,
            in_specs=[any_spec] * 5,
            out_specs=[vmem_spec] * 7,
            scratch_shapes=[
                vmem(blocks, slots, width, width),
                vmem(blocks, width, width),
                vmem(blocks, width),
                pltpu.SMEM((blocks, slots), jnp.int32),
                pltpu.SMEM((blocks,), jnp.int32),
                vmem(blocks, width, LANES),
                vmem(blocks, width, LANES),
                vmem(BAND + 1, blocks, width),
                vmem(BAND + 1, blocks, width),
                vmem(blocks, width),
                vmem(blocks, width),
                vmem(blocks * slots, width),
                vmem(BAND + 1, blocks, width),
                vmem(BAND + 1, blocks, width),
                vmem(BAND + 1, blocks, width),
                vmem(BAND + 1, blocks, width),
                vmem(DOTS, LANES),
                vmem(1, width),
                vmem(blocks, width),
                vmem(n, LANES),
                dma((blocks * slots,)),
                dma((blocks,)),
                dma((3,)),
                dma((4 * BAND,)),
                dma((4 * BAND,)),
                dma((BAND + 1,)),
                dma(()),
                dma(()),
                dma(()),
                pltpu.SemaphoreType.REGULAR((2,)),
            ],
            compiler_params=pltpu.CompilerParams(
                collective_id=0, has_side_effects=True, vmem_limit_bytes=60 << 20
            ),
        )(right_side, schur_tiles, block_cols, tile_counts, jacobi_inverse)
        return one * p - two * q, rhs - one * s + two * w

    return jax.shard_map(
        on_device,
        mesh=mesh,
        in_specs=(
            P(AXIS, None),
            P(AXIS, None, None, None),
            P(AXIS, None),
            P(AXIS),
            P(AXIS, None, None),
        ),
        out_specs=(P(AXIS, None), P(AXIS, None)),
        check_vma=False,
    )
```

```python
import functools
import itertools

import jax
import jax.numpy as jnp
from jax import lax
from jax.experimental import pallas as pl
from jax.experimental.pallas import tpu as pltpu
from jax.sharding import PartitionSpec as P

MESH = pl.DeviceIdType.MESH
LANES = 128
ROWS = 32
NEAR = 8
BAND = 2
DOTS = 4
SIZES = {128: (4, 4, 4, 2), 16: (1, 2, 4, 2)}
AXIS = "cams"


def lane_groups(width):
    return [(start, min(start + LANES, width)) for start in range(0, width, LANES)]


def fold_rows(value):
    rows, width = value.shape
    return jnp.sum(value.reshape(rows // 8, 8, width), axis=0)


def two_sum(a, b):
    total = a + b
    part = total - a
    return total, (a - (total - part)) + (b - part)


def split(a):
    wide = 4097.0 * a
    high = wide - (wide - a)
    return high, a - high


def two_product(a, b):
    product = a * b
    a_high, a_low = split(a)
    b_high, b_low = split(b)
    error = ((a_high * b_high - product) + a_high * b_low + a_low * b_high) + a_low * b_low
    return product, error


def sum_pairs(ref):
    parts = [(ref[at : at + 8, :], None) for at in range(0, ref.shape[0], 8)]

    def add(first, second):
        total, error = two_sum(first[0], second[0])
        for extra in (first[1], second[1]):
            error = error if extra is None else error + extra
        return total, error

    while len(parts) > 1:
        parts = [add(parts[i], parts[i + 1]) for i in range(0, len(parts), 2)]
    part = parts[0]
    for shift in (4, 2, 1):
        part = add(part, tuple(pltpu.roll(half, shift, 0) for half in part))
    return part[0][0:1, :], part[1][0:1, :]


def all_peers(n, me):
    sizes = SIZES[n]
    moved, stride = [], n
    for size in sizes:
        stride //= size
        place = lax.rem(lax.div(me, stride), size)
        moved.append([lax.rem(place + step, size) * stride for step in range(size)])
    offsets = list(itertools.product(*[range(size) for size in sizes]))[1:]

    def due(offset):
        hops = sum(min(o, s - o) for o, s in zip(offset[:-1], sizes[:-1]))
        return (offset[:3] != (2, 1, 0), offset[1:3] != (1, 0), offset[2] != 0, hops)

    for offset in sorted(offsets, key=due):
        yield sum(axis[step] for axis, step in zip(moved[1:], offset[1:])) + moved[0][offset[0]]


def kernel(
    n,
    rhs_hbm,
    tiles_hbm,
    cols_hbm,
    counts_hbm,
    minv_hbm,
    p_out,
    q_out,
    s_out,
    w_out,
    rhs_out,
    one_out,
    two_out,
    tiles,
    minv,
    rhs,
    cols,
    counts,
    p_col,
    q_col,
    p_ext,
    q_ext,
    s_row,
    w_row,
    prods,
    p_low,
    q_low,
    p_got,
    q_got,
    dots,
    cross,
    mid_p,
    mid_q,
    mid_low,
    everyone,
    tile_sem,
    minv_sem,
    small_sem,
    halo_send,
    halo_recv,
    mid_send,
    mid_recv,
    all_send,
    all_recv,
    ready,
):
    blocks, slots, width, _ = tiles.shape
    far = n // NEAR
    me = lax.axis_index(AXIS)
    mine = lax.rem(me, NEAR)
    plane = lax.div(me, NEAR)
    groups = lane_groups(width)
    chunks = width // ROWS

    small = [
        pltpu.make_async_copy(rhs_hbm, rhs, small_sem.at[0]),
        pltpu.make_async_copy(cols_hbm, cols, small_sem.at[1]),
        pltpu.make_async_copy(counts_hbm, counts, small_sem.at[2]),
    ]
    minv_copy = [
        pltpu.make_async_copy(minv_hbm.at[g], minv.at[g], minv_sem.at[g]) for g in range(blocks)
    ]
    tile_copy = {
        (g, k): pltpu.make_async_copy(
            tiles_hbm.at[g, k], tiles.at[g, k], tile_sem.at[g * slots + k]
        )
        for g in range(blocks)
        for k in range(slots)
    }
    def start_tiles(g):
        for k in range(1, slots):
            tile_copy[g, k].start()

    small[0].start()
    for copy in minv_copy:
        copy.start()
    start_tiles(0)

    def ahead(steps):
        return (lax.rem(me + n + steps, n),)

    def near_peer(steps):
        return (plane * NEAR + lax.rem(mine + NEAR + steps, NEAR),)

    def far_peer(steps):
        return (lax.rem(plane + far + steps, far) * NEAR + mine,)

    def ring_peers(axis):
        size = SIZES[n][axis]
        stride = 1 if axis == 1 else SIZES[n][1]
        place = lax.rem(lax.div(plane, stride), size)
        for step in range(1, size):
            moved = plane + (lax.rem(place + step, size) - place) * stride
            yield (moved * NEAR + mine,)

    line = lax.rem(plane, SIZES[n][1])
    first = line == 0
    last = line == SIZES[n][1] - 1
    relayed = first & (mine < BAND)

    barrier = pltpu.get_barrier_semaphore()

    def enter(peer):
        pl.semaphore_signal(barrier, inc=1, device_id=peer, device_id_type=MESH)

    @pl.when(mine == 0)
    def _():
        enter(ahead(-1))

    @pl.when(mine < BAND)
    def _():
        enter(ahead(-2))

    @pl.when(last & (mine < BAND))
    def _():
        enter(ahead(NEAR))

    @pl.when(jnp.logical_not(last) & (mine >= NEAR - 2))
    def _():
        enter(ahead(2))

    @pl.when(jnp.logical_not(last) & (mine == NEAR - 1))
    def _():
        enter(ahead(1))

    peers = [near_peer(s) for s in range(1, NEAR)]
    peers += [*ring_peers(0), *ring_peers(1)]
    for peer in peers:
        enter(peer)
    links = jnp.where(mine == 0, jnp.where(first, 1, 2), 0) + jnp.where(mine == 1, 1, 0)
    links = links + jnp.where(mine == NEAR - 2, 1, 0) + jnp.where(mine == NEAR - 1, 2, 0)

    def send(index, source, target, steps):
        return pltpu.make_async_remote_copy(
            src_ref=source,
            dst_ref=target,
            send_sem=halo_send.at[index],
            recv_sem=halo_recv.at[index],
            device_id=ahead(steps),
            device_id_type=MESH,
        )

    def eye(chunk):
        offset = (chunk * ROWS) % LANES
        lane = lax.broadcasted_iota(jnp.int32, (ROWS, LANES), 1)
        row = lax.broadcasted_iota(jnp.int32, (ROWS, LANES), 0)
        return lane == row + offset

    eyes = [eye(c) for c in range(LANES // ROWS)]

    def times_rows(terms, column, row_out):
        sums = [jnp.zeros((8, LANES), jnp.float32) for _ in groups]
        for c in range(chunks):
            rows = slice(c * ROWS, (c + 1) * ROWS)
            total = None
            for matrix, vector in terms:
                part = matrix[rows, :] * vector
                total = part if total is None else total + part
            value = jnp.sum(total, axis=1, keepdims=True)
            wide = jnp.broadcast_to(value, (ROWS, LANES))
            if column is not None:
                column[rows, :] = wide
            at = c * ROWS // LANES
            sums[at] = sums[at] + fold_rows(jnp.where(eyes[c % len(eyes)], wide, 0.0))
        for (low, high), value in zip(groups, sums):
            row_out[:, low:high] = jnp.sum(value, axis=0, keepdims=True)[:, : high - low]

    def times_columns(matrices, column, row_outs):
        sums = [[None for _ in groups] for _ in matrices]
        for c in range(chunks):
            rows = slice(c * ROWS, (c + 1) * ROWS)
            wide = column[rows, :]
            for index, matrix in enumerate(matrices):
                for at, (low, high) in enumerate(groups):
                    part = fold_rows(matrix[rows, low:high] * wide[:, : high - low])
                    before = sums[index][at]
                    sums[index][at] = part if before is None else before + part
        for index, row_out in enumerate(row_outs):
            for (low, high), value in zip(groups, sums[index]):
                row_out[:, low:high] = jnp.sum(value, axis=0, keepdims=True)

    start_tiles(1)
    small[1].start()
    small[2].start()
    small[0].wait()
    for g in range(blocks):
        minv_copy[g].wait()
        if g + 2 < blocks:
            start_tiles(g + 2)
        times_rows(
            [(minv.at[g], rhs[g : g + 1, :])], p_col.at[g], p_ext.at[0, g : g + 1, :]
        )

    pl.semaphore_wait(barrier, len(peers) + links)
    p_sends = [send(d - 1, p_ext.at[0], p_ext.at[d], -d) for d in range(1, BAND + 1)]

    def relay(index, source, target, recv, peer):
        return pltpu.make_async_remote_copy(
            src_ref=source,
            dst_ref=target,
            send_sem=mid_send.at[index],
            recv_sem=recv,
            device_id=peer,
            device_id_type=MESH,
        )

    def relay_in():
        return relay(0, p_ext.at[0], mid_p, mid_recv.at[0], ahead(-NEAR))

    def relay_out(distance, place):
        return relay(
            distance,
            mid_p,
            p_ext.at[distance],
            halo_recv.at[distance - 1],
            (plane * NEAR + place,),
        )

    @pl.when(relayed)
    def _():
        relay_in().start()

    direct = [jnp.logical_not(first & (mine < d)) for d in range(1, BAND + 1)]
    for copy, sent in zip(p_sends, direct):

        @pl.when(sent)
        def _(copy=copy):
            copy.start()

    for peer in ring_peers(1):
        pl.semaphore_signal(ready.at[0], inc=1, device_id=peer, device_id_type=MESH)

    small[1].wait()
    small[2].wait()
    total_blocks = n * blocks
    places = {}
    lives = {}
    for g in range(blocks):
        for k in range(1, slots):
            local = lax.rem(cols[g, k] - me * blocks + total_blocks, total_blocks)
            live = k < counts[g]
            places[g, k] = jnp.where(live, local, 0)
            lives[g, k] = live

    row_ids = lax.broadcasted_iota(jnp.int32, (blocks, width), 0)

    def spread(distance):
        total = jnp.zeros((blocks, width), jnp.float32)
        for (g, k), place in places.items():
            slot = g * slots + k
            hit = row_ids == jnp.where(lives[g, k], place - distance * blocks, -1)
            total = total + jnp.where(hit, prods[slot : slot + 1, :], 0.0)
        return total

    def picked(ext, g, k):
        place = places[g, k]
        row = ext[lax.div(place, blocks), pl.ds(lax.rem(place, blocks), 1), :]
        return jnp.where(lives[g, k], row, 0.0)

    def slot_row(g, k):
        slot = g * slots + k
        return prods.at[slot : slot + 1, :]

    for g in range(blocks):
        for k in range(1, slots):
            tile_copy[g, k].wait()
        tile_copy[g, 0].start()
        times_columns(
            [tiles.at[g, k] for k in range(1, slots)],
            p_col.at[g],
            [slot_row(g, k) for k in range(1, slots)],
        )
    for d in range(1, BAND + 1):
        p_low[d] = spread(d)
    low_sends = [send(BAND + d - 1, p_low.at[d], p_got.at[d], d) for d in range(1, BAND + 1)]
    for copy in low_sends:
        copy.start()
    p_low[0] = spread(0)

    @pl.when(last & (mine == 0))
    def _():
        relay_in().wait_recv()
        relay_out(1, NEAR - 1).start()
        relay_out(2, NEAR - 2).start()

    @pl.when(last & (mine == 1))
    def _():
        relay_in().wait_recv()
        relay_out(2, NEAR - 1).start()

    for g in range(blocks):
        tile_copy[g, 0].wait()
        times_columns([tiles.at[g, 0]], p_col.at[g], [w_row.at[g : g + 1, :]])
    w_row[...] = w_row[...] + p_low[0]
    for copy in p_sends:
        copy.wait_recv()
    for g in range(blocks):
        terms = [(tiles.at[g, k], picked(p_ext, g, k)) for k in range(1, slots)]
        times_rows(terms, None, s_row.at[g : g + 1, :])
    s_near = s_row[...] + w_row[...]
    for copy in low_sends:
        copy.wait_recv()
    s_row[...] = s_near + p_got[1] + p_got[2]

    for g in range(blocks):
        times_rows(
            [(minv.at[g], s_row[g : g + 1, :])], q_col.at[g], q_ext.at[0, g : g + 1, :]
        )
    def half_q():
        return relay(BAND + 1, q_ext.at[0], mid_q, mid_recv.at[BAND + 1], ahead(-NEAR))

    def half_low(distance, place):
        return relay(
            BAND + 1 + distance,
            q_low.at[distance],
            mid_low.at[distance],
            mid_recv.at[distance],
            (plane * NEAR + place,),
        )

    half_there = first & (plane != 0)
    half_here = last & (plane != n // NEAR - 1)

    @pl.when(half_there & (mine < BAND))
    def _():
        half_q().start()

    q_sends = [send(2 * BAND + d - 1, q_ext.at[0], q_ext.at[d], -d) for d in range(1, BAND + 1)]
    for copy in q_sends:
        copy.start()

    def put_dot(index, value):
        whole = jnp.sum(jnp.sum(value, axis=0, keepdims=True), axis=1, keepdims=True)
        dots[index : index + 1, :] = jnp.broadcast_to(whole, (1, LANES))

    for g in range(blocks):
        times_columns(
            [tiles.at[g, k] for k in range(1, slots)],
            q_col.at[g],
            [slot_row(g, k) for k in range(1, slots)],
        )
    for d in range(1, BAND + 1):
        q_low[d] = spread(d)

    @pl.when(half_here & (mine == NEAR - 1))
    def _():
        half_low(1, 0).start()
        half_low(2, 1).start()

    @pl.when(half_here & (mine == NEAR - 2))
    def _():
        half_low(2, 0).start()

    q_low_sends = [
        send(3 * BAND + d - 1, q_low.at[d], q_got.at[d], d) for d in range(1, BAND + 1)
    ]
    for copy in q_low_sends:
        copy.start()
    pl.semaphore_wait(ready.at[0], SIZES[n][1] - 1)
    for d in range(1, NEAR):
        pl.semaphore_signal(ready.at[1], inc=1, device_id=near_peer(d), device_id_type=MESH)
    put_dot(0, rhs[...] * p_ext[0])
    put_dot(1, p_ext[0] * s_row[...])
    put_dot(2, s_row[...] * q_ext[0])

    q_low[0] = spread(0)
    for g in range(blocks):
        times_columns([tiles.at[g, 0]], q_col.at[g], [w_row.at[g : g + 1, :]])
    cross[...] = jnp.sum(
        q_ext[0] * (2.0 * q_low[0] + w_row[...]), axis=0, keepdims=True
    )
    w_row[...] = w_row[...] + q_low[0]

    def add_cross(rows, low):
        cross[...] = cross[...] + 2.0 * jnp.sum(rows * low, axis=0, keepdims=True)

    here = [(mine < NEAR - 3) | (mine == NEAR - 2), mine < NEAR - 4]
    edge = jnp.logical_not(half_there)
    both_there = (edge & (mine == 0)) | (mine == NEAR - 2)
    one_there = (edge & (mine == 1)) | (mine == NEAR - 1)
    got_there = [both_there, both_there | one_there]
    for copy, wanted, d in zip(q_sends, here, range(1, BAND + 1)):

        @pl.when(wanted)
        def _(copy=copy, d=d):
            copy.wait_recv()
            add_cross(q_ext[d], q_low[d])

    for copy, wanted, d in zip(q_low_sends, got_there, range(1, BAND + 1)):

        @pl.when(wanted)
        def _(copy=copy, d=d):
            copy.wait_recv()
            add_cross(q_ext[0], q_got[d])

    @pl.when(half_here & (mine == 0))
    def _():
        half_q().wait_recv()
        half_low(1, 0).wait_recv()
        half_low(2, 0).wait_recv()
        add_cross(mid_q[...], mid_low[1] + mid_low[2])

    @pl.when(half_here & (mine == 1))
    def _():
        half_q().wait_recv()
        half_low(2, 1).wait_recv()
        add_cross(mid_q[...], mid_low[2])

    put_dot(3, cross[...])
    lane = lax.broadcasted_iota(jnp.int32, (1, LANES), 1)
    mixed = dots[0:1, :]
    for index in range(1, DOTS):
        mixed = jnp.where(lane < index * (LANES // DOTS), mixed, dots[index : index + 1, :])
    everyone[pl.ds(me, 1), :] = mixed
    pl.semaphore_wait(ready.at[1], NEAR - 1)
    for peer in all_peers(n, me):
        pltpu.make_async_remote_copy(
            src_ref=everyone.at[pl.ds(me, 1), :],
            dst_ref=everyone.at[pl.ds(me, 1), :],
            send_sem=all_send,
            recv_sem=all_recv,
            device_id=(peer,),
            device_id_type=MESH,
        ).start()
    others = everyone.at[pl.ds(0, n - 1), :]

    p_out[...] = p_ext[0]
    q_out[...] = q_ext[0]
    s_out[...] = s_row[...]
    rhs_out[...] = rhs[...]
    for copy, wanted in zip(q_sends, here):

        @pl.when(jnp.logical_not(wanted))
        def _(copy=copy):
            copy.wait_recv()

    for g in range(blocks):
        terms = [(tiles.at[g, k], picked(q_ext, g, k)) for k in range(1, slots)]
        times_rows(terms, None, s_row_up(prods, g))
    up = prods[0:blocks, :]
    for copy, wanted in zip(q_low_sends, got_there):

        @pl.when(jnp.logical_not(wanted))
        def _(copy=copy):
            copy.wait_recv()

    w_row[...] = w_row[...] + up + q_got[1] + q_got[2]

    pltpu.make_async_copy(others, others, all_recv).wait()
    high, low = sum_pairs(everyone)

    def dot(index):
        first = lane == index * (LANES // DOTS)
        return [
            jnp.sum(jnp.where(first, part, 0.0), axis=1, keepdims=True) for part in (high, low)
        ]

    (rz, rz_low), (ps, ps_low), (sq, sq_low), (qw, qw_low) = [dot(i) for i in range(DOTS)]

    def ratio(top, top_low):
        value = top / ps
        product, error = two_product(value, ps)
        return value, ((top - product) - error + (top_low - value * ps_low)) / ps

    alpha, alpha_low = ratio(rz, rz_low)
    gamma, gamma_low = ratio(sq, sq_low)
    product, error = two_product(alpha, sq)
    upper = (product - ps) + (error + (alpha * sq_low - ps_low) + alpha_low * sq)
    product, error = two_product(gamma, sq)
    lower = (qw - product) - (error - qw_low + gamma * sq_low + gamma_low * sq)
    two = upper / lower
    one = alpha + two * gamma
    one_out[...] = jnp.broadcast_to(one, (blocks, width))
    two_out[...] = jnp.broadcast_to(two, (blocks, width))
    w_out[...] = w_row[...]

    for copy in low_sends + q_sends + q_low_sends:
        copy.wait_send()
    pltpu.make_async_copy(others, others, all_send).wait()

    for copy, sent in zip(p_sends, direct):

        @pl.when(sent)
        def _(copy=copy):
            copy.wait_send()

    @pl.when(relayed)
    def _():
        relay_in().wait_send()

    @pl.when(last & (mine == 0))
    def _():
        relay_out(1, NEAR - 1).wait_send()
        relay_out(2, NEAR - 2).wait_send()

    @pl.when(last & (mine == 1))
    def _():
        relay_out(2, NEAR - 1).wait_send()

    @pl.when(half_there & (mine < BAND))
    def _():
        half_q().wait_send()

    @pl.when(half_here & (mine == NEAR - 1))
    def _():
        half_low(1, 0).wait_send()
        half_low(2, 1).wait_send()

    @pl.when(half_here & (mine == NEAR - 2))
    def _():
        half_low(2, 0).wait_send()


def s_row_up(ref, g):
    return ref.at[g : g + 1, :]


def solution(mesh):
    n = mesh.shape[AXIS]

    def on_device(right_side, schur_tiles, block_cols, tile_counts, jacobi_inverse):
        blocks, slots, width, _ = schur_tiles.shape
        dma = pltpu.SemaphoreType.DMA

        def vmem(*shape):
            return pltpu.VMEM(shape, jnp.float32)

        any_spec = pl.BlockSpec(memory_space=pl.ANY)
        vmem_spec = pl.BlockSpec(memory_space=pltpu.VMEM)
        p, q, s, w, rhs, one, two = pl.pallas_call(
            functools.partial(kernel, n),
            out_shape=[vmem(blocks, width)] * 7,
            in_specs=[any_spec] * 5,
            out_specs=[vmem_spec] * 7,
            scratch_shapes=[
                vmem(blocks, slots, width, width),
                vmem(blocks, width, width),
                vmem(blocks, width),
                pltpu.SMEM((blocks, slots), jnp.int32),
                pltpu.SMEM((blocks,), jnp.int32),
                vmem(blocks, width, LANES),
                vmem(blocks, width, LANES),
                vmem(BAND + 1, blocks, width),
                vmem(BAND + 1, blocks, width),
                vmem(blocks, width),
                vmem(blocks, width),
                vmem(blocks * slots, width),
                vmem(BAND + 1, blocks, width),
                vmem(BAND + 1, blocks, width),
                vmem(BAND + 1, blocks, width),
                vmem(BAND + 1, blocks, width),
                vmem(DOTS, LANES),
                vmem(1, width),
                vmem(blocks, width),
                vmem(blocks, width),
                vmem(BAND + 1, blocks, width),
                vmem(n, LANES),
                dma((blocks * slots,)),
                dma((blocks,)),
                dma((3,)),
                dma((4 * BAND,)),
                dma((4 * BAND,)),
                dma((2 * BAND + 2,)),
                dma((BAND + 2,)),
                dma(()),
                dma(()),
                pltpu.SemaphoreType.REGULAR((2,)),
            ],
            compiler_params=pltpu.CompilerParams(
                collective_id=0, has_side_effects=True, vmem_limit_bytes=60 << 20
            ),
        )(right_side, schur_tiles, block_cols, tile_counts, jacobi_inverse)
        return one * p - two * q, rhs - one * s + two * w

    return jax.shard_map(
        on_device,
        mesh=mesh,
        in_specs=(
            P(AXIS, None),
            P(AXIS, None, None, None),
            P(AXIS, None),
            P(AXIS),
            P(AXIS, None, None),
        ),
        out_specs=(P(AXIS, None), P(AXIS, None)),
        check_vma=False,
    )
```

```python
import functools
import itertools

import jax
import jax.numpy as jnp
from jax import lax
from jax.experimental import pallas as pl
from jax.experimental.pallas import tpu as pltpu
from jax.sharding import PartitionSpec as P

MESH = pl.DeviceIdType.MESH
LANES = 128
ROWS = 32
NEAR = 8
BAND = 2
DOTS = 4
SIZES = {128: (4, 4, 4, 2), 16: (1, 2, 4, 2)}
AXIS = "cams"


def lane_groups(width):
    return [(start, min(start + LANES, width)) for start in range(0, width, LANES)]


def fold_rows(value):
    total = value[0:8, :]
    for at in range(8, value.shape[0], 8):
        total = total + value[at : at + 8, :]
    return total


def two_sum(a, b):
    total = a + b
    part = total - a
    return total, (a - (total - part)) + (b - part)


def split(a):
    wide = 4097.0 * a
    high = wide - (wide - a)
    return high, a - high


def two_product(a, b):
    product = a * b
    a_high, a_low = split(a)
    b_high, b_low = split(b)
    error = ((a_high * b_high - product) + a_high * b_low + a_low * b_high) + a_low * b_low
    return product, error


def sum_pairs(ref):
    parts = [(ref[at : at + 8, :], None) for at in range(0, ref.shape[0], 8)]

    def add(first, second):
        total, error = two_sum(first[0], second[0])
        for extra in (first[1], second[1]):
            error = error if extra is None else error + extra
        return total, error

    while len(parts) > 1:
        parts = [add(parts[i], parts[i + 1]) for i in range(0, len(parts), 2)]
    part = parts[0]
    for shift in (4, 2, 1):
        part = add(part, tuple(pltpu.roll(half, shift, 0) for half in part))
    return part[0][0:1, :], part[1][0:1, :]


def all_peers(n, me):
    sizes = SIZES[n]
    moved, stride = [], n
    for size in sizes:
        stride //= size
        place = lax.rem(lax.div(me, stride), size)
        moved.append([lax.rem(place + step, size) * stride for step in range(size)])
    offsets = list(itertools.product(*[range(size) for size in sizes]))[1:]

    def due(offset):
        hops = sum(min(o, s - o) for o, s in zip(offset[:-1], sizes[:-1]))
        return (offset[:3] != (2, 1, 0), offset[1:3] != (1, 0), offset[2] != 0, hops)

    for offset in sorted(offsets, key=due):
        yield sum(axis[step] for axis, step in zip(moved[1:], offset[1:])) + moved[0][offset[0]]


def kernel(
    n,
    rhs_hbm,
    tiles_hbm,
    cols_hbm,
    counts_hbm,
    minv_hbm,
    p_out,
    q_out,
    s_out,
    w_out,
    rhs_out,
    one_out,
    two_out,
    tiles,
    minv,
    rhs,
    cols,
    counts,
    p_col,
    q_col,
    p_ext,
    q_ext,
    s_row,
    w_row,
    prods,
    lows,
    p_got,
    q_got,
    dots,
    cross,
    mid_p,
    mid_q,
    mid_low,
    everyone,
    tile_sem,
    minv_sem,
    small_sem,
    halo_send,
    halo_recv,
    mid_send,
    mid_recv,
    all_send,
    all_recv,
    ready,
):
    blocks, slots, width, _ = tiles.shape
    p_low, q_low = lows.at[pl.ds(0, BAND + 1)], lows.at[pl.ds(BAND + 1, BAND + 1)]
    far = n // NEAR
    me = lax.axis_index(AXIS)
    mine = lax.rem(me, NEAR)
    plane = lax.div(me, NEAR)
    groups = lane_groups(width)
    chunks = width // ROWS

    small = [
        pltpu.make_async_copy(rhs_hbm, rhs, small_sem.at[0]),
        pltpu.make_async_copy(cols_hbm, cols, small_sem.at[1]),
        pltpu.make_async_copy(counts_hbm, counts, small_sem.at[2]),
    ]
    minv_copy = [
        pltpu.make_async_copy(minv_hbm.at[g], minv.at[g], minv_sem.at[g]) for g in range(blocks)
    ]
    tile_copy = [
        pltpu.make_async_copy(
            tiles_hbm.at[g, pl.ds(1, slots - 1)], tiles.at[g, pl.ds(1, slots - 1)], tile_sem.at[g]
        )
        for g in range(blocks)
    ]
    diag_copy = [
        pltpu.make_async_copy(tiles_hbm.at[g, 0], tiles.at[g, 0], tile_sem.at[blocks])
        for g in range(blocks)
    ]

    small[0].start()
    for copy in minv_copy:
        copy.start()
    tile_copy[0].start()

    def ahead(steps):
        return (lax.rem(me + n + steps, n),)

    def near_peer(steps):
        return (plane * NEAR + lax.rem(mine + NEAR + steps, NEAR),)

    def far_peer(steps):
        return (lax.rem(plane + far + steps, far) * NEAR + mine,)

    def ring_peers(axis):
        size = SIZES[n][axis]
        stride = 1 if axis == 1 else SIZES[n][1]
        place = lax.rem(lax.div(plane, stride), size)
        for step in range(1, size):
            moved = plane + (lax.rem(place + step, size) - place) * stride
            yield (moved * NEAR + mine,)

    line = lax.rem(plane, SIZES[n][1])
    first = line == 0
    last = line == SIZES[n][1] - 1
    relayed = first & (mine < BAND)

    barrier = pltpu.get_barrier_semaphore()

    def enter(peer):
        pl.semaphore_signal(barrier, inc=1, device_id=peer, device_id_type=MESH)

    @pl.when(mine == 0)
    def _():
        enter(ahead(-1))

    @pl.when(mine < BAND)
    def _():
        enter(ahead(-2))

    @pl.when(last & (mine < BAND))
    def _():
        enter(ahead(NEAR))

    @pl.when(jnp.logical_not(last) & (mine >= NEAR - 2))
    def _():
        enter(ahead(2))

    @pl.when(jnp.logical_not(last) & (mine == NEAR - 1))
    def _():
        enter(ahead(1))

    peers = [near_peer(s) for s in range(1, NEAR)]
    peers += [*ring_peers(0), *ring_peers(1)]
    for peer in peers:
        enter(peer)
    links = jnp.where(mine == 0, jnp.where(first, 1, 2), 0) + jnp.where(mine == 1, 1, 0)
    links = links + jnp.where(mine == NEAR - 2, 1, 0) + jnp.where(mine == NEAR - 1, 2, 0)

    def send(index, source, target, steps):
        return pltpu.make_async_remote_copy(
            src_ref=source,
            dst_ref=target,
            send_sem=halo_send.at[min(index, BAND)],
            recv_sem=halo_recv.at[index],
            device_id=ahead(steps),
            device_id_type=MESH,
        )

    def eye(chunk):
        offset = (chunk * ROWS) % LANES
        lane = lax.broadcasted_iota(jnp.int32, (ROWS, LANES), 1)
        row = lax.broadcasted_iota(jnp.int32, (ROWS, LANES), 0)
        return lane == row + offset

    eyes = [eye(c) for c in range(LANES // ROWS)]

    def times_rows(terms, column, row_out):
        sums = [jnp.zeros((8, LANES), jnp.float32) for _ in groups]
        for c in range(chunks):
            rows = slice(c * ROWS, (c + 1) * ROWS)
            total = None
            for matrix, vector in terms:
                part = matrix[rows, :] * vector
                total = part if total is None else total + part
            value = jnp.sum(total, axis=1, keepdims=True)
            wide = jnp.broadcast_to(value, (ROWS, LANES))
            if column is not None:
                column[rows, :] = wide
            at = c * ROWS // LANES
            sums[at] = sums[at] + fold_rows(jnp.where(eyes[c % len(eyes)], wide, 0.0))
        for (low, high), value in zip(groups, sums):
            row_out[:, low:high] = jnp.sum(value, axis=0, keepdims=True)[:, : high - low]

    def times_columns(matrices, column, row_outs):
        sums = [[None for _ in groups] for _ in matrices]
        for c in range(chunks):
            rows = slice(c * ROWS, (c + 1) * ROWS)
            wide = column[rows, :]
            for index, matrix in enumerate(matrices):
                for at, (low, high) in enumerate(groups):
                    part = fold_rows(matrix[rows, low:high] * wide[:, : high - low])
                    before = sums[index][at]
                    sums[index][at] = part if before is None else before + part
        for index, row_out in enumerate(row_outs):
            for (low, high), value in zip(groups, sums[index]):
                row_out[:, low:high] = jnp.sum(value, axis=0, keepdims=True)

    tile_copy[1].start()
    small[1].start()
    small[2].start()
    small[0].wait()
    for g in range(blocks):
        minv_copy[g].wait()
        if g + 2 < blocks:
            tile_copy[g + 2].start()
        times_rows(
            [(minv.at[g], rhs[g : g + 1, :])], p_col.at[g], p_ext.at[0, g : g + 1, :]
        )

    pl.semaphore_wait(barrier, len(peers) + links)
    p_sends = [send(d - 1, p_ext.at[0], p_ext.at[d], -d) for d in range(1, BAND + 1)]

    def relay(index, source, target, recv, peer):
        return pltpu.make_async_remote_copy(
            src_ref=source,
            dst_ref=target,
            send_sem=mid_send.at[index],
            recv_sem=recv,
            device_id=peer,
            device_id_type=MESH,
        )

    def relay_in():
        return relay(0, p_ext.at[0], mid_p, mid_recv.at[0], ahead(-NEAR))

    def relay_out(distance, place):
        return relay(
            distance,
            mid_p,
            p_ext.at[distance],
            halo_recv.at[distance - 1],
            (plane * NEAR + place,),
        )

    @pl.when(relayed)
    def _():
        relay_in().start()

    direct = [jnp.logical_not(first & (mine < d)) for d in range(1, BAND + 1)]
    for copy, sent in zip(p_sends, direct):

        @pl.when(sent)
        def _(copy=copy):
            copy.start()

    for peer in ring_peers(1):
        pl.semaphore_signal(ready.at[0], inc=1, device_id=peer, device_id_type=MESH)

    small[1].wait()
    small[2].wait()
    total_blocks = n * blocks
    places = {}
    lives = {}
    for g in range(blocks):
        for k in range(1, slots):
            local = lax.rem(cols[g, k] - me * blocks + total_blocks, total_blocks)
            live = k < counts[g]
            places[g, k] = jnp.where(live, local, 0)
            lives[g, k] = live

    row_ids = lax.broadcasted_iota(jnp.int32, (blocks, width), 0)

    def spread(distance):
        total = jnp.zeros((blocks, width), jnp.float32)
        for (g, k), place in places.items():
            slot = g * slots + k
            hit = row_ids == jnp.where(lives[g, k], place - distance * blocks, -1)
            total = total + jnp.where(hit, prods[slot : slot + 1, :], 0.0)
        return total

    def picked(ext, g, k):
        place = places[g, k]
        row = ext[lax.div(place, blocks), pl.ds(lax.rem(place, blocks), 1), :]
        return jnp.where(lives[g, k], row, 0.0)

    def slot_row(g, k):
        slot = g * slots + k
        return prods.at[slot : slot + 1, :]

    for g in range(blocks):
        tile_copy[g].wait()
        diag_copy[g].start()
        times_columns(
            [tiles.at[g, k] for k in range(1, slots)],
            p_col.at[g],
            [slot_row(g, k) for k in range(1, slots)],
        )
    for d in range(1, BAND + 1):
        p_low[d] = spread(d)
    low_sends = [send(BAND + d - 1, p_low.at[d], p_got.at[d], d) for d in range(1, BAND + 1)]
    for copy in low_sends:
        copy.start()
    p_low[0] = spread(0)

    @pl.when(last & (mine == 0))
    def _():
        relay_in().wait_recv()
        relay_out(1, NEAR - 1).start()
        relay_out(2, NEAR - 2).start()

    @pl.when(last & (mine == 1))
    def _():
        relay_in().wait_recv()
        relay_out(2, NEAR - 1).start()

    diagonals = tiles.at[pl.ds(0, blocks), 0]
    pltpu.make_async_copy(diagonals, diagonals, tile_sem.at[blocks]).wait()
    for g in range(blocks):
        times_columns([tiles.at[g, 0]], p_col.at[g], [w_row.at[g : g + 1, :]])
    w_row[...] = w_row[...] + p_low[0]
    for copy in p_sends:
        copy.wait_recv()
    for g in range(blocks):
        terms = [(tiles.at[g, k], picked(p_ext, g, k)) for k in range(1, slots)]
        times_rows(terms, None, s_row.at[g : g + 1, :])
    s_near = s_row[...] + w_row[...]
    for copy in low_sends:
        copy.wait_recv()
    s_row[...] = s_near + p_got[1] + p_got[2]

    for g in range(blocks):
        times_rows(
            [(minv.at[g], s_row[g : g + 1, :])], q_col.at[g], q_ext.at[0, g : g + 1, :]
        )
    def half_q():
        return relay(0, q_ext.at[0], mid_q, mid_recv.at[BAND + 1], ahead(-NEAR))

    def half_low(distance, place):
        return relay(
            distance,
            q_low.at[distance],
            mid_low.at[distance],
            mid_recv.at[distance],
            (plane * NEAR + place,),
        )

    half_there = first & (plane != 0)
    half_here = last & (plane != n // NEAR - 1)

    @pl.when(relayed)
    def _():
        relay_in().wait_send()

    @pl.when(half_there & (mine < BAND))
    def _():
        half_q().start()

    q_sends = [send(2 * BAND + d - 1, q_ext.at[0], q_ext.at[d], -d) for d in range(1, BAND + 1)]
    for copy in q_sends:
        copy.start()

    def put_dot(index, value):
        whole = jnp.sum(jnp.sum(value, axis=0, keepdims=True), axis=1, keepdims=True)
        dots[index : index + 1, :] = jnp.broadcast_to(whole, (1, LANES))

    for g in range(blocks):
        times_columns(
            [tiles.at[g, k] for k in range(1, slots)],
            q_col.at[g],
            [slot_row(g, k) for k in range(1, slots)],
        )
    for d in range(1, BAND + 1):
        q_low[d] = spread(d)

    @pl.when(half_here & (mine == NEAR - 1))
    def _():
        half_low(1, 0).start()
        half_low(2, 1).start()

    @pl.when(half_here & (mine == NEAR - 2))
    def _():
        half_low(2, 0).start()

    q_low_sends = [
        send(3 * BAND + d - 1, q_low.at[d], q_got.at[d], d) for d in range(1, BAND + 1)
    ]
    for copy in q_low_sends:
        copy.start()
    pl.semaphore_wait(ready.at[0], SIZES[n][1] - 1)
    for d in range(1, NEAR):
        pl.semaphore_signal(ready.at[1], inc=1, device_id=near_peer(d), device_id_type=MESH)
    put_dot(0, rhs[...] * p_ext[0])
    put_dot(1, p_ext[0] * s_row[...])
    put_dot(2, s_row[...] * q_ext[0])

    q_low[0] = spread(0)
    for g in range(blocks):
        times_columns([tiles.at[g, 0]], q_col.at[g], [w_row.at[g : g + 1, :]])
    cross[...] = jnp.sum(
        q_ext[0] * (2.0 * q_low[0] + w_row[...]), axis=0, keepdims=True
    )
    w_row[...] = w_row[...] + q_low[0]

    def add_cross(rows, low):
        cross[...] = cross[...] + 2.0 * jnp.sum(rows * low, axis=0, keepdims=True)

    here = [(mine < NEAR - 3) | (mine == NEAR - 2), mine < NEAR - 4]
    edge = jnp.logical_not(half_there)
    both_there = (edge & (mine == 0)) | (mine == NEAR - 2)
    one_there = (edge & (mine == 1)) | (mine == NEAR - 1)
    got_there = [both_there, both_there | one_there]
    for copy, wanted, d in zip(q_sends, here, range(1, BAND + 1)):

        @pl.when(wanted)
        def _(copy=copy, d=d):
            copy.wait_recv()
            add_cross(q_ext[d], q_low[d])

    for copy, wanted, d in zip(q_low_sends, got_there, range(1, BAND + 1)):

        @pl.when(wanted)
        def _(copy=copy, d=d):
            copy.wait_recv()
            add_cross(q_ext[0], q_got[d])

    @pl.when(half_here & (mine == 0))
    def _():
        half_q().wait_recv()
        half_low(1, 0).wait_recv()
        half_low(2, 0).wait_recv()
        add_cross(mid_q[...], mid_low[1] + mid_low[2])

    @pl.when(half_here & (mine == 1))
    def _():
        half_q().wait_recv()
        half_low(2, 1).wait_recv()
        add_cross(mid_q[...], mid_low[2])

    put_dot(3, cross[...])
    lane = lax.broadcasted_iota(jnp.int32, (1, LANES), 1)
    mixed = dots[0:1, :]
    for index in range(1, DOTS):
        mixed = jnp.where(lane < index * (LANES // DOTS), mixed, dots[index : index + 1, :])
    everyone[pl.ds(me, 1), :] = mixed
    pl.semaphore_wait(ready.at[1], NEAR - 1)
    for peer in all_peers(n, me):
        pltpu.make_async_remote_copy(
            src_ref=everyone.at[pl.ds(me, 1), :],
            dst_ref=everyone.at[pl.ds(me, 1), :],
            send_sem=all_send,
            recv_sem=all_recv,
            device_id=(peer,),
            device_id_type=MESH,
        ).start()
    others = everyone.at[pl.ds(0, n - 1), :]

    p_out[...] = p_ext[0]
    q_out[...] = q_ext[0]
    s_out[...] = s_row[...]
    rhs_out[...] = rhs[...]
    for copy, wanted in zip(q_sends, here):

        @pl.when(jnp.logical_not(wanted))
        def _(copy=copy):
            copy.wait_recv()

    for g in range(blocks):
        terms = [(tiles.at[g, k], picked(q_ext, g, k)) for k in range(1, slots)]
        times_rows(terms, None, s_row_up(prods, g))
    up = prods[0:blocks, :]
    for copy, wanted in zip(q_low_sends, got_there):

        @pl.when(jnp.logical_not(wanted))
        def _(copy=copy):
            copy.wait_recv()

    w_row[...] = w_row[...] + up + q_got[1] + q_got[2]

    pltpu.make_async_copy(others, others, all_recv).wait()
    high, low = sum_pairs(everyone)

    def dot(index):
        first = lane == index * (LANES // DOTS)
        return [
            jnp.sum(jnp.where(first, part, 0.0), axis=1, keepdims=True) for part in (high, low)
        ]

    (rz, rz_low), (ps, ps_low), (sq, sq_low), (qw, qw_low) = [dot(i) for i in range(DOTS)]

    def ratio(top, top_low):
        value = top / ps
        product, error = two_product(value, ps)
        return value, ((top - product) - error + (top_low - value * ps_low)) / ps

    alpha, alpha_low = ratio(rz, rz_low)
    gamma, gamma_low = ratio(sq, sq_low)
    product, error = two_product(alpha, sq)
    upper = (product - ps) + (error + (alpha * sq_low - ps_low) + alpha_low * sq)
    product, error = two_product(gamma, sq)
    lower = (qw - product) - (error - qw_low + gamma * sq_low + gamma_low * sq)
    two = upper / lower
    one = alpha + two * gamma
    one_out[...] = jnp.broadcast_to(one, (blocks, width))
    two_out[...] = jnp.broadcast_to(two, (blocks, width))
    w_out[...] = w_row[...]

    assert len(low_sends + q_sends + q_low_sends) == lows.shape[0]
    pltpu.make_async_copy(lows, lows, halo_send.at[BAND]).wait()
    pltpu.make_async_copy(others, others, all_send).wait()

    for copy, sent in zip(p_sends, direct):

        @pl.when(sent)
        def _(copy=copy):
            copy.wait_send()

    @pl.when(last & (mine == 0))
    def _():
        relay_out(1, NEAR - 1).wait_send()
        relay_out(2, NEAR - 2).wait_send()

    @pl.when(last & (mine == 1))
    def _():
        relay_out(2, NEAR - 1).wait_send()

    @pl.when(half_there & (mine < BAND))
    def _():
        half_q().wait_send()

    @pl.when(half_here & (mine == NEAR - 1))
    def _():
        half_low(1, 0).wait_send()
        half_low(2, 1).wait_send()

    @pl.when(half_here & (mine == NEAR - 2))
    def _():
        half_low(2, 0).wait_send()


def s_row_up(ref, g):
    return ref.at[g : g + 1, :]


def solution(mesh):
    n = mesh.shape[AXIS]

    def on_device(right_side, schur_tiles, block_cols, tile_counts, jacobi_inverse):
        blocks, slots, width, _ = schur_tiles.shape
        dma = pltpu.SemaphoreType.DMA

        def vmem(*shape):
            return pltpu.VMEM(shape, jnp.float32)

        any_spec = pl.BlockSpec(memory_space=pl.ANY)
        vmem_spec = pl.BlockSpec(memory_space=pltpu.VMEM)
        p, q, s, w, rhs, one, two = pl.pallas_call(
            functools.partial(kernel, n),
            out_shape=[vmem(blocks, width)] * 7,
            in_specs=[any_spec] * 5,
            out_specs=[vmem_spec] * 7,
            scratch_shapes=[
                vmem(blocks, slots, width, width),
                vmem(blocks, width, width),
                vmem(blocks, width),
                pltpu.SMEM((blocks, slots), jnp.int32),
                pltpu.SMEM((blocks,), jnp.int32),
                vmem(blocks, width, LANES),
                vmem(blocks, width, LANES),
                vmem(BAND + 1, blocks, width),
                vmem(BAND + 1, blocks, width),
                vmem(blocks, width),
                vmem(blocks, width),
                vmem(blocks * slots, width),
                vmem(2 * BAND + 2, blocks, width),
                vmem(BAND + 1, blocks, width),
                vmem(BAND + 1, blocks, width),
                vmem(DOTS, LANES),
                vmem(1, width),
                vmem(blocks, width),
                vmem(blocks, width),
                vmem(BAND + 1, blocks, width),
                vmem(n, LANES),
                dma((blocks + 1,)),
                dma((blocks,)),
                dma((3,)),
                dma((BAND + 1,)),
                dma((4 * BAND,)),
                dma((BAND + 1,)),
                dma((BAND + 2,)),
                dma(()),
                dma(()),
                pltpu.SemaphoreType.REGULAR((2,)),
            ],
            compiler_params=pltpu.CompilerParams(
                collective_id=0, has_side_effects=True, vmem_limit_bytes=60 << 20
            ),
        )(right_side, schur_tiles, block_cols, tile_counts, jacobi_inverse)
        return one * p - two * q, rhs - one * s + two * w

    return jax.shard_map(
        on_device,
        mesh=mesh,
        in_specs=(
            P(AXIS, None),
            P(AXIS, None, None, None),
            P(AXIS, None),
            P(AXIS),
            P(AXIS, None, None),
        ),
        out_specs=(P(AXIS, None), P(AXIS, None)),
        check_vma=False,
    )
```

```python
import functools
import itertools

import jax
import jax.numpy as jnp
from jax import lax
from jax.experimental import pallas as pl
from jax.experimental.pallas import tpu as pltpu
from jax.sharding import PartitionSpec as P

MESH = pl.DeviceIdType.MESH
LANES = 128
ROWS = 32
NEAR = 8
BAND = 2
DOTS = 4
SIZES = {128: (4, 4, 4, 2), 32: (2, 2, 4, 2)}
AXIS = "cams"


def lane_groups(width):
    return [(start, min(start + LANES, width)) for start in range(0, width, LANES)]


def fold_rows(value):
    total = value[0:8, :]
    for at in range(8, value.shape[0], 8):
        total = total + value[at : at + 8, :]
    return total


def two_sum(a, b):
    total = a + b
    part = total - a
    return total, (a - (total - part)) + (b - part)


def split(a):
    wide = 4097.0 * a
    high = wide - (wide - a)
    return high, a - high


def two_product(a, b):
    product = a * b
    a_high, a_low = split(a)
    b_high, b_low = split(b)
    error = ((a_high * b_high - product) + a_high * b_low + a_low * b_high) + a_low * b_low
    return product, error


def sum_pairs(ref):
    parts = [(ref[at : at + 8, :], None) for at in range(0, ref.shape[0], 8)]

    def add(first, second):
        total, error = two_sum(first[0], second[0])
        for extra in (first[1], second[1]):
            error = error if extra is None else error + extra
        return total, error

    while len(parts) > 1:
        parts = [add(parts[i], parts[i + 1]) for i in range(0, len(parts), 2)]
    part = parts[0]
    for shift in (4, 2, 1):
        part = add(part, tuple(pltpu.roll(half, shift, 0) for half in part))
    return part[0][0:1, :], part[1][0:1, :]


def all_peers(n, me):
    sizes = SIZES[n]
    moved, stride = [], n
    for size in sizes:
        stride //= size
        place = lax.rem(lax.div(me, stride), size)
        moved.append([lax.rem(place + step, size) * stride for step in range(size)])
    offsets = list(itertools.product(*[range(size) for size in sizes]))[1:]

    def due(offset):
        hops = sum(min(o, s - o) for o, s in zip(offset[:-1], sizes[:-1]))
        return (offset[:3] != (1, 1, 0), offset[1:3] != (1, 0), offset[2] != 0, hops)

    for offset in sorted(offsets, key=due):
        yield sum(axis[step] for axis, step in zip(moved[1:], offset[1:])) + moved[0][offset[0]]


def kernel(
    n,
    rhs_hbm,
    tiles_hbm,
    cols_hbm,
    counts_hbm,
    minv_hbm,
    p_out,
    q_out,
    s_out,
    w_out,
    rhs_out,
    one_out,
    two_out,
    tiles,
    minv,
    rhs,
    cols,
    counts,
    p_col,
    q_col,
    p_ext,
    q_ext,
    s_row,
    w_row,
    prods,
    lows,
    p_got,
    q_got,
    dots,
    cross,
    mid_p,
    mid_q,
    mid_low,
    everyone,
    tile_sem,
    minv_sem,
    small_sem,
    halo_send,
    halo_recv,
    mid_send,
    mid_recv,
    all_send,
    all_recv,
    ready,
):
    blocks, slots, width, _ = tiles.shape
    p_low, q_low = lows.at[pl.ds(0, BAND + 1)], lows.at[pl.ds(BAND + 1, BAND + 1)]
    far = n // NEAR
    me = lax.axis_index(AXIS)
    mine = lax.rem(me, NEAR)
    plane = lax.div(me, NEAR)
    groups = lane_groups(width)
    chunks = width // ROWS

    small = [
        pltpu.make_async_copy(rhs_hbm, rhs, small_sem.at[0]),
        pltpu.make_async_copy(cols_hbm, cols, small_sem.at[1]),
        pltpu.make_async_copy(counts_hbm, counts, small_sem.at[2]),
    ]
    minv_copy = [
        pltpu.make_async_copy(minv_hbm.at[g], minv.at[g], minv_sem.at[g]) for g in range(blocks)
    ]
    tile_copy = [
        pltpu.make_async_copy(
            tiles_hbm.at[g, pl.ds(1, slots - 1)], tiles.at[g, pl.ds(1, slots - 1)], tile_sem.at[g]
        )
        for g in range(blocks)
    ]
    diag_copy = [
        pltpu.make_async_copy(tiles_hbm.at[g, 0], tiles.at[g, 0], tile_sem.at[blocks])
        for g in range(blocks)
    ]

    small[0].start()
    for copy in minv_copy:
        copy.start()
    tile_copy[0].start()

    def ahead(steps):
        return (lax.rem(me + n + steps, n),)

    def near_peer(steps):
        return (plane * NEAR + lax.rem(mine + NEAR + steps, NEAR),)

    def far_peer(steps):
        return (lax.rem(plane + far + steps, far) * NEAR + mine,)

    def ring_peers(axis):
        size = SIZES[n][axis]
        stride = 1 if axis == 1 else SIZES[n][1]
        place = lax.rem(lax.div(plane, stride), size)
        for step in range(1, size):
            moved = plane + (lax.rem(place + step, size) - place) * stride
            yield (moved * NEAR + mine,)

    lines = SIZES[n][1]
    line = lax.rem(plane, lines)
    first = line == 0
    last = line == lines - 1
    relayed = first & (mine < BAND)

    barrier = pltpu.get_barrier_semaphore()

    def enter(peer):
        pl.semaphore_signal(barrier, inc=1, device_id=peer, device_id_type=MESH)

    @pl.when(mine == 0)
    def _():
        enter(ahead(-1))

    @pl.when(mine < BAND)
    def _():
        enter(ahead(-2))

    @pl.when(last & (mine < BAND))
    def _():
        enter(ahead(NEAR))

    @pl.when(jnp.logical_not(last) & (mine >= NEAR - 2))
    def _():
        enter(ahead(2))

    @pl.when(jnp.logical_not(last) & (mine == NEAR - 1))
    def _():
        enter(ahead(1))

    peers = [near_peer(s) for s in range(1, NEAR)]
    peers += [*ring_peers(0), *ring_peers(1)]
    for peer in peers:
        enter(peer)
    links = jnp.where(mine == 0, jnp.where(first, 1, 2), 0) + jnp.where(mine == 1, 1, 0)
    links = links + jnp.where(mine == NEAR - 2, 1, 0) + jnp.where(mine == NEAR - 1, 2, 0)

    def send(index, source, target, steps):
        return pltpu.make_async_remote_copy(
            src_ref=source,
            dst_ref=target,
            send_sem=halo_send.at[min(index, BAND)],
            recv_sem=halo_recv.at[index],
            device_id=ahead(steps),
            device_id_type=MESH,
        )

    def eye(chunk):
        offset = (chunk * ROWS) % LANES
        lane = lax.broadcasted_iota(jnp.int32, (ROWS, LANES), 1)
        row = lax.broadcasted_iota(jnp.int32, (ROWS, LANES), 0)
        return lane == row + offset

    eyes = [eye(c) for c in range(LANES // ROWS)]

    def times_rows(terms, column, row_out):
        sums = [jnp.zeros((8, LANES), jnp.float32) for _ in groups]
        for c in range(chunks):
            rows = slice(c * ROWS, (c + 1) * ROWS)
            total = None
            for matrix, vector in terms:
                part = matrix[rows, :] * vector
                total = part if total is None else total + part
            value = jnp.sum(total, axis=1, keepdims=True)
            wide = jnp.broadcast_to(value, (ROWS, LANES))
            if column is not None:
                column[rows, :] = wide
            at = c * ROWS // LANES
            sums[at] = sums[at] + fold_rows(jnp.where(eyes[c % len(eyes)], wide, 0.0))
        for (low, high), value in zip(groups, sums):
            row_out[:, low:high] = jnp.sum(value, axis=0, keepdims=True)[:, : high - low]

    def times_columns(matrices, column, row_outs):
        sums = [[None for _ in groups] for _ in matrices]
        for c in range(chunks):
            rows = slice(c * ROWS, (c + 1) * ROWS)
            wide = column[rows, :]
            for index, matrix in enumerate(matrices):
                for at, (low, high) in enumerate(groups):
                    part = fold_rows(matrix[rows, low:high] * wide[:, : high - low])
                    before = sums[index][at]
                    sums[index][at] = part if before is None else before + part
        for index, row_out in enumerate(row_outs):
            for (low, high), value in zip(groups, sums[index]):
                row_out[:, low:high] = jnp.sum(value, axis=0, keepdims=True)

    tile_copy[1].start()
    small[1].start()
    small[2].start()
    small[0].wait()
    for g in range(blocks):
        minv_copy[g].wait()
        if g + 2 < blocks:
            tile_copy[g + 2].start()
        times_rows(
            [(minv.at[g], rhs[g : g + 1, :])], p_col.at[g], p_ext.at[0, g : g + 1, :]
        )

    pl.semaphore_wait(barrier, len(peers) + links)
    p_sends = [send(d - 1, p_ext.at[0], p_ext.at[d], -d) for d in range(1, BAND + 1)]

    def relay(index, source, target, recv, peer):
        return pltpu.make_async_remote_copy(
            src_ref=source,
            dst_ref=target,
            send_sem=mid_send.at[index],
            recv_sem=recv,
            device_id=peer,
            device_id_type=MESH,
        )

    def relay_in():
        return relay(0, p_ext.at[0], mid_p, mid_recv.at[0], ahead(-NEAR))

    def relay_out(distance, place):
        return relay(
            distance,
            mid_p,
            p_ext.at[distance],
            halo_recv.at[distance - 1],
            (plane * NEAR + place,),
        )

    @pl.when(relayed)
    def _():
        relay_in().start()

    direct = [jnp.logical_not(first & (mine < d)) for d in range(1, BAND + 1)]
    for copy, sent in zip(p_sends, direct):

        @pl.when(sent)
        def _(copy=copy):
            copy.start()

    for peer in ring_peers(1):
        pl.semaphore_signal(ready.at[0], inc=1, device_id=peer, device_id_type=MESH)

    small[1].wait()
    small[2].wait()
    total_blocks = n * blocks
    places = {}
    lives = {}
    for g in range(blocks):
        for k in range(1, slots):
            local = lax.rem(cols[g, k] - me * blocks + total_blocks, total_blocks)
            live = k < counts[g]
            places[g, k] = jnp.where(live, local, 0)
            lives[g, k] = live

    row_ids = lax.broadcasted_iota(jnp.int32, (blocks, width), 0)

    def spread(distance):
        total = jnp.zeros((blocks, width), jnp.float32)
        for (g, k), place in places.items():
            slot = g * slots + k
            hit = row_ids == jnp.where(lives[g, k], place - distance * blocks, -1)
            total = total + jnp.where(hit, prods[slot : slot + 1, :], 0.0)
        return total

    def picked(ext, g, k):
        place = places[g, k]
        row = ext[lax.div(place, blocks), pl.ds(lax.rem(place, blocks), 1), :]
        return jnp.where(lives[g, k], row, 0.0)

    def slot_row(g, k):
        slot = g * slots + k
        return prods.at[slot : slot + 1, :]

    for g in range(blocks):
        tile_copy[g].wait()
        diag_copy[g].start()
        times_columns(
            [tiles.at[g, k] for k in range(1, slots)],
            p_col.at[g],
            [slot_row(g, k) for k in range(1, slots)],
        )
    for d in range(1, BAND + 1):
        p_low[d] = spread(d)
    low_sends = [send(BAND + d - 1, p_low.at[d], p_got.at[d], d) for d in range(1, BAND + 1)]
    for copy in low_sends:
        copy.start()
    p_low[0] = spread(0)

    @pl.when(last & (mine == 0))
    def _():
        relay_in().wait_recv()
        relay_out(1, NEAR - 1).start()
        relay_out(2, NEAR - 2).start()

    @pl.when(last & (mine == 1))
    def _():
        relay_in().wait_recv()
        relay_out(2, NEAR - 1).start()

    diagonals = tiles.at[pl.ds(0, blocks), 0]
    pltpu.make_async_copy(diagonals, diagonals, tile_sem.at[blocks]).wait()
    for g in range(blocks):
        times_columns([tiles.at[g, 0]], p_col.at[g], [w_row.at[g : g + 1, :]])
    w_row[...] = w_row[...] + p_low[0]
    for copy in p_sends:
        copy.wait_recv()
    for g in range(blocks):
        terms = [(tiles.at[g, k], picked(p_ext, g, k)) for k in range(1, slots)]
        times_rows(terms, None, s_row.at[g : g + 1, :])
    s_near = s_row[...] + w_row[...]
    for copy in low_sends:
        copy.wait_recv()
    s_row[...] = s_near + p_got[1] + p_got[2]

    for g in range(blocks):
        times_rows(
            [(minv.at[g], s_row[g : g + 1, :])], q_col.at[g], q_ext.at[0, g : g + 1, :]
        )
    def half_q():
        peer = (jnp.where(outer_there, plane + lines - 1, plane - 1) * NEAR + mine,)
        return relay(0, q_ext.at[0], mid_q, mid_recv.at[BAND + 1], peer)

    def half_low(distance, place):
        return relay(
            distance,
            q_low.at[distance],
            mid_low.at[distance],
            mid_recv.at[distance],
            (jnp.where(outer_from, plane + lines, plane) * NEAR + place,),
        )

    half_there = first & (plane != 0)
    half_from = last & (plane != n // NEAR - 1)
    outer_from = plane == n // NEAR - lines - 1
    outer_there = plane == n // NEAR - lines
    half_here = last & jnp.logical_not(outer_from)

    @pl.when(relayed)
    def _():
        relay_in().wait_send()

    @pl.when(half_there & (mine < BAND))
    def _():
        half_q().start()

    q_sends = [send(2 * BAND + d - 1, q_ext.at[0], q_ext.at[d], -d) for d in range(1, BAND + 1)]
    for copy in q_sends:
        copy.start()

    def put_dot(index, value):
        whole = jnp.sum(jnp.sum(value, axis=0, keepdims=True), axis=1, keepdims=True)
        dots[index : index + 1, :] = jnp.broadcast_to(whole, (1, LANES))

    for g in range(blocks):
        times_columns(
            [tiles.at[g, k] for k in range(1, slots)],
            q_col.at[g],
            [slot_row(g, k) for k in range(1, slots)],
        )
    for d in range(1, BAND + 1):
        q_low[d] = spread(d)

    @pl.when(half_from & (mine == NEAR - 1))
    def _():
        half_low(1, 0).start()
        half_low(2, 1).start()

    @pl.when(half_from & (mine == NEAR - 2))
    def _():
        half_low(2, 0).start()

    q_low_sends = [
        send(3 * BAND + d - 1, q_low.at[d], q_got.at[d], d) for d in range(1, BAND + 1)
    ]
    for copy in q_low_sends:
        copy.start()
    pl.semaphore_wait(ready.at[0], SIZES[n][1] - 1)
    for d in range(1, NEAR):
        pl.semaphore_signal(ready.at[1], inc=1, device_id=near_peer(d), device_id_type=MESH)
    put_dot(0, rhs[...] * p_ext[0])
    put_dot(1, p_ext[0] * s_row[...])
    put_dot(2, s_row[...] * q_ext[0])

    q_low[0] = spread(0)
    for g in range(blocks):
        times_columns([tiles.at[g, 0]], q_col.at[g], [w_row.at[g : g + 1, :]])
    cross[...] = jnp.sum(
        q_ext[0] * (2.0 * q_low[0] + w_row[...]), axis=0, keepdims=True
    )
    w_row[...] = w_row[...] + q_low[0]

    def add_cross(rows, low):
        cross[...] = cross[...] + 2.0 * jnp.sum(rows * low, axis=0, keepdims=True)

    here = [(mine < NEAR - 3) | (mine == NEAR - 2), mine < NEAR - 4]
    edge = jnp.logical_not(half_there)
    both_there = (edge & (mine == 0)) | (mine == NEAR - 2)
    one_there = (edge & (mine == 1)) | (mine == NEAR - 1)
    got_there = [both_there, both_there | one_there]
    for copy, wanted, d in zip(q_sends, here, range(1, BAND + 1)):

        @pl.when(wanted)
        def _(copy=copy, d=d):
            copy.wait_recv()
            add_cross(q_ext[d], q_low[d])

    for copy, wanted, d in zip(q_low_sends, got_there, range(1, BAND + 1)):

        @pl.when(wanted)
        def _(copy=copy, d=d):
            copy.wait_recv()
            add_cross(q_ext[0], q_got[d])

    @pl.when(half_here & (mine == 0))
    def _():
        half_q().wait_recv()
        half_low(1, 0).wait_recv()
        half_low(2, 0).wait_recv()
        add_cross(mid_q[...], mid_low[1] + mid_low[2])

    @pl.when(half_here & (mine == 1))
    def _():
        half_q().wait_recv()
        half_low(2, 1).wait_recv()
        add_cross(mid_q[...], mid_low[2])

    put_dot(3, cross[...])
    lane = lax.broadcasted_iota(jnp.int32, (1, LANES), 1)
    mixed = dots[0:1, :]
    for index in range(1, DOTS):
        mixed = jnp.where(lane < index * (LANES // DOTS), mixed, dots[index : index + 1, :])
    everyone[pl.ds(me, 1), :] = mixed
    pl.semaphore_wait(ready.at[1], NEAR - 1)
    for peer in all_peers(n, me):
        pltpu.make_async_remote_copy(
            src_ref=everyone.at[pl.ds(me, 1), :],
            dst_ref=everyone.at[pl.ds(me, 1), :],
            send_sem=all_send,
            recv_sem=all_recv,
            device_id=(peer,),
            device_id_type=MESH,
        ).start()
    others = everyone.at[pl.ds(0, n - 1), :]

    p_out[...] = p_ext[0]
    q_out[...] = q_ext[0]
    s_out[...] = s_row[...]
    rhs_out[...] = rhs[...]
    for copy, wanted in zip(q_sends, here):

        @pl.when(jnp.logical_not(wanted))
        def _(copy=copy):
            copy.wait_recv()

    for g in range(blocks):
        terms = [(tiles.at[g, k], picked(q_ext, g, k)) for k in range(1, slots)]
        times_rows(terms, None, s_row_up(prods, g))
    up = prods[0:blocks, :]
    for copy, wanted in zip(q_low_sends, got_there):

        @pl.when(jnp.logical_not(wanted))
        def _(copy=copy):
            copy.wait_recv()

    w_row[...] = w_row[...] + up + q_got[1] + q_got[2]

    pltpu.make_async_copy(others, others, all_recv).wait()
    high, low = sum_pairs(everyone)

    def dot(index):
        first = lane == index * (LANES // DOTS)
        return [
            jnp.sum(jnp.where(first, part, 0.0), axis=1, keepdims=True) for part in (high, low)
        ]

    (rz, rz_low), (ps, ps_low), (sq, sq_low), (qw, qw_low) = [dot(i) for i in range(DOTS)]

    def ratio(top, top_low):
        value = top / ps
        product, error = two_product(value, ps)
        return value, ((top - product) - error + (top_low - value * ps_low)) / ps

    alpha, alpha_low = ratio(rz, rz_low)
    gamma, gamma_low = ratio(sq, sq_low)
    product, error = two_product(alpha, sq)
    upper = (product - ps) + (error + (alpha * sq_low - ps_low) + alpha_low * sq)
    product, error = two_product(gamma, sq)
    lower = (qw - product) - (error - qw_low + gamma * sq_low + gamma_low * sq)
    two = upper / lower
    one = alpha + two * gamma
    one_out[...] = jnp.broadcast_to(one, (blocks, width))
    two_out[...] = jnp.broadcast_to(two, (blocks, width))
    w_out[...] = w_row[...]

    assert len(low_sends + q_sends + q_low_sends) == lows.shape[0]
    pltpu.make_async_copy(lows, lows, halo_send.at[BAND]).wait()
    pltpu.make_async_copy(others, others, all_send).wait()

    for copy, sent in zip(p_sends, direct):

        @pl.when(sent)
        def _(copy=copy):
            copy.wait_send()

    @pl.when(last & (mine == 0))
    def _():
        relay_out(1, NEAR - 1).wait_send()
        relay_out(2, NEAR - 2).wait_send()

    @pl.when(last & (mine == 1))
    def _():
        relay_out(2, NEAR - 1).wait_send()

    @pl.when(half_there & (mine < BAND))
    def _():
        half_q().wait_send()

    @pl.when(half_from & (mine == NEAR - 1))
    def _():
        half_low(1, 0).wait_send()
        half_low(2, 1).wait_send()

    @pl.when(half_from & (mine == NEAR - 2))
    def _():
        half_low(2, 0).wait_send()


def s_row_up(ref, g):
    return ref.at[g : g + 1, :]


def solution(mesh):
    n = mesh.shape[AXIS]

    def on_device(right_side, schur_tiles, block_cols, tile_counts, jacobi_inverse):
        blocks, slots, width, _ = schur_tiles.shape
        dma = pltpu.SemaphoreType.DMA

        def vmem(*shape):
            return pltpu.VMEM(shape, jnp.float32)

        any_spec = pl.BlockSpec(memory_space=pl.ANY)
        vmem_spec = pl.BlockSpec(memory_space=pltpu.VMEM)
        p, q, s, w, rhs, one, two = pl.pallas_call(
            functools.partial(kernel, n),
            out_shape=[vmem(blocks, width)] * 7,
            in_specs=[any_spec] * 5,
            out_specs=[vmem_spec] * 7,
            scratch_shapes=[
                vmem(blocks, slots, width, width),
                vmem(blocks, width, width),
                vmem(blocks, width),
                pltpu.SMEM((blocks, slots), jnp.int32),
                pltpu.SMEM((blocks,), jnp.int32),
                vmem(blocks, width, LANES),
                vmem(blocks, width, LANES),
                vmem(BAND + 1, blocks, width),
                vmem(BAND + 1, blocks, width),
                vmem(blocks, width),
                vmem(blocks, width),
                vmem(blocks * slots, width),
                vmem(2 * BAND + 2, blocks, width),
                vmem(BAND + 1, blocks, width),
                vmem(BAND + 1, blocks, width),
                vmem(DOTS, LANES),
                vmem(1, width),
                vmem(blocks, width),
                vmem(blocks, width),
                vmem(BAND + 1, blocks, width),
                vmem(n, LANES),
                dma((blocks + 1,)),
                dma((blocks,)),
                dma((3,)),
                dma((BAND + 1,)),
                dma((4 * BAND,)),
                dma((BAND + 1,)),
                dma((BAND + 2,)),
                dma(()),
                dma(()),
                pltpu.SemaphoreType.REGULAR((2,)),
            ],
            compiler_params=pltpu.CompilerParams(
                collective_id=0, has_side_effects=True, vmem_limit_bytes=60 << 20
            ),
        )(right_side, schur_tiles, block_cols, tile_counts, jacobi_inverse)
        return one * p - two * q, rhs - one * s + two * w

    return jax.shard_map(
        on_device,
        mesh=mesh,
        in_specs=(
            P(AXIS, None),
            P(AXIS, None, None, None),
            P(AXIS, None),
            P(AXIS),
            P(AXIS, None, None),
        ),
        out_specs=(P(AXIS, None), P(AXIS, None)),
        check_vma=False,
    )
```
